256 devices in a mesh: sub: 128 (over x, y, z_hi, core), panel: 2 (over z_lo).
Axes of the slice: x: 4, y: 4, z: 8 (z_hi: 4, z_lo: 2; z = z_hi * 2 + z_lo), core: 2. Of those that a mesh axis runs over, the one named last changes fastest.
Arguments:
- solution: float32 [131072, 256], P('sub', 'panel'), may hold values from -6 to 6
- residual: float32 [131072, 256], P('sub', 'panel'), may hold values from -25 to 25
- shadow: float32 [131072, 256], P('sub', 'panel'), may hold values from -120 to 120
- direction: float32 [131072, 256], P('sub', 'panel'), may hold values from -6 to 6
- old_image: float32 [131072, 256], P('sub', 'panel'), may hold values from -6 to 6
- rho_prev: float32 [256], P('panel'), may hold values from 1 to 4
- alpha_prev: float32 [256], P('panel'), may hold values from 0.5 to 2
- omega_prev: float32 [256], P('panel'), may hold values from 0.5 to 2
- lower_inverse: bfloat16 [128, 1792, 1792], P('sub', None, 'panel'), may hold values from -0.4 to 0.4, as said below
- upper_inverse: bfloat16 [128, 1792, 1792], P('sub', None, 'panel'), may hold values from -0.4 to 0.4, as said below
- neighbours: int32 [16, 131072], P(None, 'sub'), may hold values from 0 to 1792, as said below
- edge_weight: float32 [16, 131072], P(None, 'sub'), may hold values from 0.1 to 1
- node_shift: float32 [131072], P('sub'), may hold values from 3 to 12
- send_rows: int32 [128, 2, 384], P('sub'), may hold values from 0 to 1023
Outputs:
- new_solution: float32 [131072, 256], P('sub', 'panel')
- new_residual: float32 [131072, 256], P('sub', 'panel')
- step_alpha: float32 [256], P('panel')
- step_omega: float32 [256], P('panel')
- next_rho: float32 [256], P('panel')
The draws below stay inside these ranges and needn't reach their ends.
Inputs may be any that keep to these rules, and one draw needn't show every extreme that they name: lower_inverse[s] is zero above its diagonal. upper_inverse[s] is zero below its diagonal. `neighbours`: an entry below 1024 is an owned node, from 1024 a ghost node from the lower neighbour's list, from 1408 one from the upper neighbour's list; 1792 marks an empty slot. send_rows[s, 0] lists the rows of subdomain s that subdomain s - 1 holds as ghosts, send_rows[s, 1] those that subdomain s + 1 holds, modulo 128.
All inputs are finite; a program needn't handle non-finite values.
Results may differ from the reference program's by a relative error of at most 0.0097.
Values may be sent and summed in bfloat16 or wider, within the bound.
A program may use at most 64 MiB of HBM per device.

```python
import math
import jax
import jax.numpy as jnp
from jax import lax

OWN = 1024
SRC = 256
BORDER = 384
NB = 16
SUBS = 128
NODES = 131072
EXT = 1792


def residual_pair(key):
    base_key = jax.random.fold_in(key, 17)
    subkeys = jax.random.split(base_key, 4)
    position = lax.broadcasted_iota(jnp.float32, (NODES, 1), 0) / NODES
    rough_log = jax.random.uniform(subkeys[0], (NODES, 1), jnp.float32, -1.15, 1.15)
    row_scale = 0.5 * (1.0 + 2.0 * position) * jnp.exp(rough_log)
    values = jnp.clip(jax.random.normal(subkeys[1], (NODES, SRC), jnp.float32), -5.0, 5.0)
    noise_part = jnp.clip(jax.random.normal(subkeys[2], (NODES, SRC), jnp.float32), -5.0, 5.0)
    spread = jnp.exp(jax.random.uniform(subkeys[3], (1, SRC), jnp.float32, -1.2, 1.2))
    residual_part = row_scale * values
    return (residual_part, residual_part + spread * row_scale * noise_part)


def draw_residual(key, part):
    return residual_pair(key)[0]


def draw_shadow(key, part):
    return residual_pair(key)[1]


def triangle(key, below):
    subkeys = jax.random.split(key, 2)
    row_index = lax.broadcasted_iota(jnp.int32, (1, EXT, 1), 1)
    col_index = lax.broadcasted_iota(jnp.int32, (1, 1, EXT), 2)
    coupling = jnp.clip(jax.random.normal(subkeys[0], (SUBS, EXT, EXT), jnp.float32), -5.0, 5.0) * (0.4 / math.sqrt(EXT))
    diagonal = jax.random.uniform(subkeys[1], (SUBS, EXT, 1), jnp.float32, 0.7, 1.3)
    if below:
        keep_mask = row_index > col_index
    else:
        keep_mask = row_index < col_index
    return 0.3 * jnp.where(row_index == col_index, diagonal, jnp.where(keep_mask, coupling, 0.0))


def draw_lower_inverse(key, part):
    return triangle(jax.random.fold_in(key, 29), True).astype(jnp.bfloat16)


def draw_upper_inverse(key, part):
    return triangle(jax.random.fold_in(key, 31), False).astype(jnp.bfloat16)


def draw_neighbours(key, part):
    subkeys = jax.random.split(jax.random.fold_in(key, 41), 2)
    degree = jax.random.randint(subkeys[0], (1, NODES), NB - NB // 4, NB + 1)
    picked = jax.random.randint(subkeys[1], (NB, NODES), 0, EXT)
    slot_index = lax.broadcasted_iota(jnp.int32, (NB, NODES), 0)
    return jnp.where(slot_index < degree, picked, EXT).astype(jnp.int32)


def touch_ends(result, stream_key, least, largest):
    dims = result.shape
    spot = [jax.random.randint(jax.random.fold_in(stream_key, axis), (), 0, dims[axis]) for axis in range(len(dims))]
    result = result.at[tuple(spot)].set(least)
    longest = dims.index(max(dims))
    spot[longest] = (spot[longest] + 1) % dims[longest]
    return result.at[tuple(spot)].set(largest)


def levels(own_key, shape, cuts, smallest, high):
    gain = 1.0
    for axis_at, parts in cuts:
        heights = jax.random.uniform(jax.random.fold_in(jax.random.fold_in(own_key, 6), axis_at), (parts,), jnp.float32, smallest / len(cuts), high / len(cuts))
        gain = gain * jnp.repeat(jnp.exp(heights), shape[axis_at] // parts).reshape((-1,) + (1,) * (len(shape) - 1 - axis_at))
    return gain


def bell_draw(rng, shape, width, bound, cuts=(), dtype=jnp.bfloat16):
    drawn = jax.random.normal(rng, shape, jnp.float32) * width
    if len(cuts) > 0:
        drawn = levels(rng, shape, cuts, -0.22, 0.18) * drawn
    return jnp.clip(drawn, min=-bound, max=bound).astype(dtype)


def setup_inputs(seed: int = 0) -> dict:
    splits = jax.random.split(jax.random.key(seed), 15)
    return {
        "solution": bell_draw(splits[0], (NODES, SRC), 1.0, 6.0, ((0, 128), (1, 2)), jnp.float32),
        "residual": draw_residual(jax.random.fold_in(splits[14], 71), 0),
        "shadow": draw_shadow(jax.random.fold_in(splits[14], 71), 0),
        "direction": bell_draw(splits[3], (NODES, SRC), 1.0, 6.0, ((0, 128), (1, 2)), jnp.float32),
        "old_image": bell_draw(splits[4], (NODES, SRC), 1.0, 6.0, ((0, 128), (1, 2)), jnp.float32),
        "rho_prev": jnp.clip(jnp.exp(math.log(4.0) - 1.3862944 * jax.random.uniform(splits[5], (SRC,), jnp.float32) ** levels(splits[5], (SRC,), ((0, 2),), -0.2, 0.2)), 1.0, 4.0),
        "alpha_prev": jnp.clip(jnp.exp(math.log(2.0) - 1.3862944 * jax.random.uniform(splits[6], (SRC,), jnp.float32) ** levels(splits[6], (SRC,), ((0, 2),), -0.2, 0.2)), 0.5, 2.0),
        "omega_prev": jnp.clip(jnp.exp(math.log(2.0) - 1.3862944 * jax.random.uniform(splits[7], (SRC,), jnp.float32) ** levels(splits[7], (SRC,), ((0, 2),), -0.2, 0.2)), 0.5, 2.0),
        "lower_inverse": draw_lower_inverse(jax.random.fold_in(splits[14], 71), 0),
        "upper_inverse": draw_upper_inverse(jax.random.fold_in(splits[14], 71), 0),
        "neighbours": draw_neighbours(jax.random.fold_in(splits[14], 71), 0),
        "edge_weight": jnp.clip(jnp.exp(math.log(1.0) - 2.3025851 * jax.random.uniform(splits[11], (NB, NODES), jnp.float32) ** levels(splits[11], (NB, NODES), ((1, 128),), -0.2, 0.2)), 0.1, 1.0),
        "node_shift": jnp.clip(jnp.exp(math.log(12.0) - 1.3862944 * jax.random.uniform(splits[12], (NODES,), jnp.float32) ** levels(splits[12], (NODES,), ((0, 128),), -0.2, 0.2)), 3.0, 12.0),
        "send_rows": touch_ends(jax.random.randint(splits[13], (SUBS, 2, BORDER), 0, OWN), jax.random.fold_in(splits[13], 1), 0, OWN - 1).astype(jnp.int32),
    }


FLOOR_SHARE = 0.3
EPSILON = 1e-06

def pick_rows(block_rows, chosen):
    return block_rows[chosen]

def extend(vector, send_rows):
    blocks = vector.reshape(SUBS, OWN, SRC)
    picked = jax.vmap(pick_rows)(blocks, send_rows)
    from_lower = jnp.roll(picked[:, 1], 1, axis=0)
    from_upper = jnp.roll(picked[:, 0], -1, axis=0)
    return jnp.concatenate([blocks, from_lower, from_upper], axis=1)

def operate(vector, send_rows, neighbours, edge_weight, node_shift):
    extended = extend(vector, send_rows)
    padded = jnp.concatenate([extended, jnp.zeros((SUBS, 1, SRC), jnp.float32)], axis=1)
    link_table = neighbours.reshape(NB, SUBS, OWN).transpose(1, 0, 2)
    weights = edge_weight.reshape(NB, SUBS, OWN).transpose(1, 0, 2)
    shifts = node_shift.reshape(SUBS, OWN)

    def one_block(block_items):
        ext_rows, link_rows, weight_rows, shift_rows = block_items
        present = jnp.where(link_rows < EXT, weight_rows, jnp.float32(0.0))
        coupled = lax.optimization_barrier(jnp.sum(present[:, :, None] * ext_rows[link_rows], axis=0))
        diagonal = shift_rows + lax.optimization_barrier(jnp.sum(present, axis=0))
        return diagonal[:, None] * ext_rows[:OWN] - coupled
    return lax.map(one_block, (padded, link_table, weights, shifts)).reshape(NODES, SRC)

def precondition(vector, send_rows, lower_inverse, upper_inverse):
    extended = extend(vector, send_rows)

    def one_block(block_items):
        ext_rows, lower_block, upper_block = block_items
        rounded = lax.optimization_barrier(ext_rows.astype(jnp.bfloat16)).astype(jnp.float32)
        inner_part = jnp.dot(lower_block.astype(jnp.float32), rounded, precision=lax.Precision.HIGHEST)
        inner_part = lax.optimization_barrier(inner_part.astype(jnp.bfloat16)).astype(jnp.float32)
        return jnp.dot(upper_block[:OWN].astype(jnp.float32), inner_part, precision=lax.Precision.HIGHEST)
    return lax.map(one_block, (extended, lower_inverse, upper_inverse)).reshape(NODES, SRC)

def column_mean(left_side, right_side):
    return lax.optimization_barrier(jnp.sum(left_side * right_side, axis=0)) / NODES

def reference(solution, residual, shadow, direction, old_image, rho_prev, alpha_prev, omega_prev, lower_inverse, upper_inverse, neighbours, edge_weight, node_shift, send_rows):
    rho_now = column_mean(shadow, residual)
    shadow_square = column_mean(shadow, shadow)
    step_beta = rho_now / rho_prev * (alpha_prev / omega_prev)
    new_direction = residual + step_beta * (direction - omega_prev * old_image)
    direction_hat = precondition(new_direction, send_rows, lower_inverse, upper_inverse)
    image_new = operate(direction_hat, send_rows, neighbours, edge_weight, node_shift)
    denominator = column_mean(shadow, image_new)
    image_square = column_mean(image_new, image_new)
    step_alpha = rho_now / jnp.maximum(denominator, FLOOR_SHARE * jnp.sqrt(shadow_square * image_square))
    middle = residual - step_alpha * image_new
    middle_hat = precondition(middle, send_rows, lower_inverse, upper_inverse)
    tested = operate(middle_hat, send_rows, neighbours, edge_weight, node_shift)
    step_omega = column_mean(tested, middle) / (column_mean(tested, tested) + EPSILON)
    new_solution = solution + step_alpha * direction_hat + step_omega * middle_hat
    new_residual = middle - step_omega * tested
    next_rho = column_mean(shadow, new_residual)
    return (new_solution, new_residual, step_alpha, step_omega, next_rho)
```

```python
import functools

import jax
import jax.numpy as jnp
from jax import lax
from jax.experimental import pallas as pl
from jax.experimental.pallas import tpu as pltpu
from jax.sharding import Mesh
from jax.sharding import PartitionSpec as P

SUB = ("sub_0", "sub_1", "sub_2", "sub_3")
FLOOR_SHARE = 0.3
EPSILON = 1e-06

OWN = 1024
EXT = 1792
HALF = 896
BORDER = 384
NB = 16
COLS = 128
CHUNK = 128
NX, NY, NZ, NC = 4, 4, 4, 2
F32 = jnp.float32
BF16 = jnp.bfloat16
MESH = pl.DeviceIdType.MESH


def dot(a, b):
    return lax.dot_general(a, b, (((1,), (0,)), ((), ())), preferred_element_type=F32)


def dot_nt(a, b):
    return lax.dot_general(a, b, (((1,), (1,)), ((), ())), preferred_element_type=F32)


def chunks(body, init=0):
    def step(i, carry):
        return body(pl.ds(pl.multiple_of(i * CHUNK, CHUNK), CHUNK), carry)

    return lax.fori_loop(0, OWN // CHUNK, step, init)


def fold(x):
    return jnp.sum(x.reshape(CHUNK // 8, 8, COLS), axis=0)


def butterfly(x):
    sub = lax.broadcasted_iota(jnp.int32, x.shape, 0)
    lane = lax.broadcasted_iota(jnp.int32, x.shape, 1) // 16
    for s in (1, 2, 4):
        down = pltpu.roll(pltpu.roll(x, s, 0), 128 - 16 * s, 1)
        up = pltpu.roll(pltpu.roll(x, 8 - s, 0), 16 * s, 1)
        sub_bit = (sub // s) % 2
        lane_bit = (lane // s) % 2
        x = jnp.where(sub_bit == lane_bit, x, jnp.where(sub_bit == 1, down, up))
    return x


def kernel(
    r_hbm, s_hbm, d_hbm, oi_hbm, sol_hbm, low_hbm, up_hbm,
    scal, nbr, ew, shift, rows_ref,
    new_sol, new_res, alpha_out, omega_out, rho_out,
    r, s, d, oi, sol, low, up,
    w_mat, sel, diag, code_t, base_t, wgt_t,
    xe, rq, sel_rq, g_rq, sel_u, g_u, ub, y, v, m, mh,
    x1_in, x2_in, p_in, u_in, y_in, p_out, u_out, y_out, inner, part,
    ar_a, ar_b,
    load_sem, g_send, g_recv, p_send, p_recv, a_send, a_recv,
):
    panel = lax.axis_index("panel")
    ix, iy, iz, ic = (lax.axis_index(name) for name in SUB)
    flat = ((ix * NY + iy) * NZ + iz) * NC + ic

    def coords(index):
        return {
            "sub_0": index // (NY * NZ * NC),
            "sub_1": (index // (NZ * NC)) % NY,
            "sub_2": (index // NC) % NZ,
            "sub_3": index % NC,
        }

    total = NX * NY * NZ * NC
    above = coords((flat + 1) % total)
    below = coords((flat + total - 1) % total)
    partner = {"panel": 1 - panel}
    plane = [
        {"sub_0": (ix + o // NY) % NX, "sub_1": (iy + o % NY) % NY} for o in range(1, NX * NY)
    ]
    column = [
        {"sub_2": (iz + o // NC) % NZ, "sub_3": (ic + o % NC) % NC} for o in range(1, NZ * NC)
    ]

    def load(src, dst, i):
        copy = pltpu.make_async_copy(src, dst, load_sem.at[i])
        copy.start()
        return copy

    loads = [
        load(s_hbm, s, 0), load(r_hbm, r, 1), load(d_hbm, d, 2), load(oi_hbm, oi, 3),
        load(low_hbm.at[0], low, 4), load(up_hbm.at[0, pl.ds(0, OWN)], up, 5), load(sol_hbm, sol, 6),
    ]

    barrier = pltpu.get_barrier_semaphore()
    peers = plane + column + [above, below, partner]
    for peer in peers:
        pl.semaphore_signal(barrier, inc=1, device_id=peer, device_id_type=MESH)

    sends = []

    def send(src, dst, ssem, rsem, peer):
        copy = pltpu.make_async_remote_copy(
            src_ref=src, dst_ref=dst, send_sem=ssem, recv_sem=rsem,
            device_id=peer, device_id_type=MESH,
        )
        copy.start()
        return copy

    def reduce_start(n, rows):
        mine = ar_a.at[n, ix * NY + iy]
        mine[...] = jnp.concatenate(rows + [jnp.zeros((8 - len(rows), COLS), F32)], axis=0)
        for o, peer in enumerate(plane):
            sends.append(send(mine, mine, a_send.at[n, o], a_recv.at[n, o], peer))
        return sends[-len(plane):]

    def reduce_middle(n, copies):
        for copy in copies:
            copy.wait_recv()
        mine = ar_b.at[n, iz * NC + ic]
        mine[...] = jnp.sum(ar_a[n], axis=0)
        for o, peer in enumerate(column):
            k = NX * NY - 1 + o
            sends.append(send(mine, mine, a_send.at[n, k], a_recv.at[n, k], peer))
        return sends[-len(column):]

    def reduce_end(n, copies):
        for copy in copies:
            copy.wait_recv()
        return jnp.sum(ar_b[n], axis=0) * (1.0 / (OWN * total))

    def ghosts_start(src, dst, k):
        a = send(src.at[pl.ds(0, BORDER)], dst.at[pl.ds(BORDER, BORDER)], g_send.at[k, 0], g_recv.at[k, 0], below)
        b = send(src.at[pl.ds(BORDER, BORDER)], dst.at[pl.ds(0, BORDER)], g_send.at[k, 1], g_recv.at[k, 1], above)
        sends.extend([a, b])
        return [a, b]

    zero = jnp.zeros((8, COLS), F32)
    loads[0].wait()
    loads[1].wait()

    def opening(at, carry):
        sr, ss = carry
        a, b = s[at, :], r[at, :]
        return sr + fold(a * b), ss + fold(a * a)

    sr, ss = chunks(opening, (zero, zero))
    pl.semaphore_wait(barrier, len(peers))
    first = reduce_start(0, [jnp.sum(sr, axis=0, keepdims=True), jnp.sum(ss, axis=0, keepdims=True)])

    lane = lax.broadcasted_iota(jnp.int32, (CHUNK, CHUNK), 1).astype(F32)
    for n in range(2 * BORDER // CHUNK):
        side, at = n // (BORDER // CHUNK), (n % (BORDER // CHUNK)) * CHUNK
        chosen = rows_ref[0, side : side + 1, at : at + CHUNK].astype(F32)
        across = jnp.transpose(jnp.broadcast_to(chosen, (CHUNK, CHUNK)))
        for t in range(OWN // CHUNK):
            sel[n * CHUNK : (n + 1) * CHUNK, t * CHUNK : (t + 1) * CHUNK] = jnp.where(
                across == lane + float(t * CHUNK), 1.0, 0.0
            ).astype(BF16)

    loads[2].wait()
    loads[3].wait()
    omega_prev = scal[2:3, :]

    def combine(at, _):
        q = d[at, :] - omega_prev * oi[at, :]
        d[at, :] = q
        rq[at, 0:COLS] = r[at, :].astype(BF16)
        rq[at, COLS : 2 * COLS] = q.astype(BF16)
        return 0

    chunks(combine)
    sel_rq[...] = dot(sel[...], rq[...]).astype(BF16)
    rq_copies = ghosts_start(sel_rq, g_rq, 0)
    second = reduce_middle(0, first)

    valid = nbr[...] < EXT
    present = jnp.sum(jnp.where(valid, ew[...], 0.0), axis=0, keepdims=True)
    for t in range(OWN // CHUNK):
        at = slice(t * CHUNK, (t + 1) * CHUNK)
        line = present[:, at] + shift[t : t + 1, :]
        diag[at, :] = jnp.transpose(jnp.broadcast_to(line, (CHUNK, CHUNK)))
        for h in range(NB // 8):
            turned = butterfly(nbr[h * 8 : h * 8 + 8, at].astype(F32))
            turned = turned.astype(jnp.int32)
            inside = lax.broadcasted_iota(jnp.int32, (8, CHUNK), 1) % 16
            here = slice(h * CHUNK, (h + 1) * CHUNK)
            code_t[t * 8 : t * 8 + 8, here] = (turned // COLS) * 16 + inside
            base_t[t * 8 : t * 8 + 8, here] = turned % COLS
            wgt_t[t * 8 : t * 8 + 8, here] = butterfly(ew[h * 8 : h * 8 + 8, at])

    blocks = EXT // COLS
    code_row = lax.broadcasted_iota(jnp.int32, (blocks * 16, 2 * CHUNK), 0)
    base_row = lax.broadcasted_iota(jnp.int32, (COLS, 2 * CHUNK), 0)

    def build(g, _):
        one = pl.ds(g, 1)
        left = jnp.where(code_row == code_t[one, :], wgt_t[one, :], 0.0).astype(BF16)
        right = jnp.where(base_row == base_t[one, :], 1.0, 0.0).astype(BF16)
        found = dot_nt(left, right).astype(BF16)
        at = pl.ds(pl.multiple_of(g * 16, 16), 16)
        for a in range(blocks):
            w_mat[at, a * COLS : (a + 1) * COLS] = found[a * 16 : (a + 1) * 16, :]
        return 0

    lax.fori_loop(0, OWN // 16, build, 0)

    def apply(n):
        x1 = xe.at[n, pl.ds(0, HALF)]
        x2 = xe.at[n, pl.ds(HALF, HALF)]
        q4 = HALF // 2

        def link(src, dst, k):
            return pltpu.make_async_remote_copy(
                src_ref=src, dst_ref=dst, send_sem=p_send.at[n, k], recv_sem=p_recv.at[n, k],
                device_id=partner, device_id_type=MESH,
            )

        give_x1 = link(x1, x1_in.at[n], 0)
        give_x2 = link(x2, x2_in.at[n], 1)
        give_p0 = link(p_out.at[n, 0], p_in.at[n, 0], 2)
        give_p1 = link(p_out.at[n, 1], p_in.at[n, 1], 3)
        give_u = link(u_out.at[n], u_in.at[n], 4)
        give_y = link(y_out.at[n], y_in.at[n], 5)

        @pl.when(panel == 0)
        def _():
            give_x2.start()

            def lower(src, dst):
                for h in range(2):
                    at = slice(h * q4, (h + 1) * q4)
                    dst[at, :] = dot(low[HALF + h * q4 : HALF + (h + 1) * q4, :], src[...]).astype(BF16)

            def upper(src, put):
                inner[0:q4, :] = dot(low[0:q4, 0:q4], src[0:q4, :]).astype(BF16)
                inner[q4:HALF, :] = dot(low[q4:HALF, :], src[...]).astype(BF16)
                put(slice(0, q4), dot(up[0:q4, :], inner[...]))
                put(slice(q4, HALF), dot(up[q4:HALF, q4:HALF], inner[q4:HALF, :]))

            lower(x1, p_out.at[n, 0])
            give_p0.start()

            def keep(at, value):
                y[at, :] = value

            upper(x1, keep)
            give_x1.wait_recv()
            lower(x1_in.at[n], p_out.at[n, 1])
            give_p1.start()

            def post(at, value):
                u_out[n, at, :] = value.astype(BF16)

            upper(x1_in.at[n], post)
            give_u.start()
            give_y.wait_recv()
            y[0:HALF, :] = y[0:HALF, :] + y_in[n, 0:HALF, :].astype(F32)
            y[HALF:OWN, :] = y_in[n, HALF:OWN, :].astype(F32)
            for copy in (give_x2, give_p0, give_p1, give_u):
                copy.wait_send()

        @pl.when(panel == 1)
        def _():
            give_x1.start()

            def lower(src, k):
                part[k, 0:q4, :] = dot(low[HALF : HALF + q4, 0:q4], src[0:q4, :])
                part[k, q4:HALF, :] = dot(low[HALF + q4 : EXT, :], src[...])

            def upper(k, put):
                inner[...] = (part[k] + p_in[n, k].astype(F32)).astype(BF16)
                for h in range(2):
                    at = slice(h * (OWN // 2), (h + 1) * (OWN // 2))
                    put(at, dot(up[at, :], inner[...]))

            lower(x2, 1)
            give_x2.wait_recv()
            lower(x2_in.at[n], 0)
            give_p0.wait_recv()

            def post(at, value):
                y_out[n, at, :] = value.astype(BF16)

            upper(0, post)
            give_y.start()
            give_p1.wait_recv()

            def keep(at, value):
                y[at, :] = value

            upper(1, keep)
            give_u.wait_recv()
            y[0:HALF, :] = y[0:HALF, :] + u_in[n].astype(F32)
            for copy in (give_x1, give_y):
                copy.wait_send()

    def operate(n, out):
        ub[...] = y[...].astype(BF16)
        sel_u[n] = dot(sel[...], ub[...]).astype(BF16)
        copies = ghosts_start(sel_u.at[n], g_u.at[n], 1 + n)
        out[...] = diag[...] * y[...] - dot(w_mat[:, 0:OWN], ub[...])
        for copy in copies:
            copy.wait_recv()
        out[...] = out[...] - dot(w_mat[:, OWN:EXT], g_u[n])

    mean = reduce_end(0, second)
    rho_now, shadow_square = mean[0:1, :], mean[1:2, :]
    step_beta = rho_now / scal[0:1, :] * (scal[1:2, :] / omega_prev)

    def direct(at, _):
        xe[0, at, :] = (r[at, :] + step_beta * d[at, :]).astype(BF16)
        return 0

    chunks(direct)
    for copy in rq_copies:
        copy.wait_recv()
    xe[0, OWN:EXT, :] = (
        g_rq[:, 0:COLS].astype(F32) + step_beta * g_rq[:, COLS : 2 * COLS].astype(F32)
    ).astype(BF16)
    loads[4].wait()
    loads[5].wait()
    apply(0)
    operate(0, v)

    def image(at, carry):
        sv, vv = carry
        a, b = s[at, :], v[at, :]
        return sv + fold(a * b), vv + fold(b * b)

    sv, vv = chunks(image, (zero, zero))
    first = reduce_start(1, [jnp.sum(sv, axis=0, keepdims=True), jnp.sum(vv, axis=0, keepdims=True)])
    ub[...] = v[...].astype(BF16)
    sel_u[2] = dot(sel[...], ub[...]).astype(BF16)
    v_copies = ghosts_start(sel_u.at[2], g_u.at[2], 3)
    loads[6].wait()
    second = reduce_middle(1, first)
    for copy in v_copies:
        copy.wait_recv()
    mean = reduce_end(1, second)
    denominator, image_square = mean[0:1, :], mean[1:2, :]
    step_alpha = rho_now / jnp.maximum(
        denominator, FLOOR_SHARE * jnp.sqrt(shadow_square * image_square)
    )
    alpha_out[...] = step_alpha

    def halfway(at, _):
        value = r[at, :] - step_alpha * v[at, :]
        m[at, :] = value
        xe[1, at, :] = value.astype(BF16)
        sol[at, :] = sol[at, :] + step_alpha * y[at, :]
        return 0

    chunks(halfway)
    xe[1, OWN:EXT, :] = (
        g_rq[:, 0:COLS].astype(F32) - step_alpha * g_u[2].astype(F32)
    ).astype(BF16)
    apply(1)
    operate(1, v)

    def closing(at, carry):
        a, b, c = s[at, :], v[at, :], m[at, :]
        tm, tt, sm, st = carry
        return tm + fold(b * c), tt + fold(b * b), sm + fold(a * c), st + fold(a * b)

    sums = chunks(closing, (zero, zero, zero, zero))
    first = reduce_start(2, [jnp.sum(x, axis=0, keepdims=True) for x in sums])
    second = reduce_middle(2, first)
    mean = reduce_end(2, second)
    step_omega = mean[0:1, :] / (mean[1:2, :] + EPSILON)
    omega_out[...] = step_omega
    rho_out[...] = mean[2:3, :] - step_omega * mean[3:4, :]

    def final(at, _):
        new_sol[at, :] = sol[at, :] + step_omega * y[at, :]
        new_res[at, :] = m[at, :] - step_omega * v[at, :]
        return 0

    chunks(final)
    for copy in sends:
        copy.wait_send()


def per_device(
    solution, residual, shadow, direction, old_image, rho_prev, alpha_prev, omega_prev,
    lower_inverse, upper_inverse, neighbours, edge_weight, node_shift, send_rows,
):
    hbm = pl.BlockSpec(memory_space=pl.ANY)
    vmem = pl.BlockSpec(memory_space=pltpu.VMEM)
    vec = pltpu.VMEM((OWN, COLS), F32)
    scal = jnp.stack([rho_prev, alpha_prev, omega_prev])
    dma = pltpu.SemaphoreType.DMA
    outs = pl.pallas_call(
        kernel,
        out_shape=[jax.ShapeDtypeStruct((OWN, COLS), F32)] * 2 + [jax.ShapeDtypeStruct((1, COLS), F32)] * 3,
        in_specs=[hbm] * 7 + [vmem] * 5,
        out_specs=[vmem] * 5,
        scratch_shapes=[vec] * 5
        + [pltpu.VMEM((EXT, HALF), BF16), pltpu.VMEM((OWN, HALF), BF16)]
        + [
            pltpu.VMEM((OWN, EXT), BF16),
            pltpu.VMEM((2 * BORDER, OWN), BF16),
            vec,
            pltpu.VMEM((OWN // 16, 256), jnp.int32),
            pltpu.VMEM((OWN // 16, 256), jnp.int32),
            pltpu.VMEM((OWN // 16, 256), F32),
        ]
        + [
            pltpu.VMEM((2, EXT, COLS), BF16),
            pltpu.VMEM((OWN, 2 * COLS), BF16),
            pltpu.VMEM((2 * BORDER, 2 * COLS), BF16),
            pltpu.VMEM((2 * BORDER, 2 * COLS), BF16),
            pltpu.VMEM((3, 2 * BORDER, COLS), BF16),
            pltpu.VMEM((3, 2 * BORDER, COLS), BF16),
            pltpu.VMEM((OWN, COLS), BF16),
            vec, vec, vec, vec,
        ]
        + [
            pltpu.VMEM((2, HALF, COLS), BF16),
            pltpu.VMEM((2, HALF, COLS), BF16),
            pltpu.VMEM((2, 2, HALF, COLS), BF16),
            pltpu.VMEM((2, HALF, COLS), BF16),
            pltpu.VMEM((2, OWN, COLS), BF16),
            pltpu.VMEM((2, 2, HALF, COLS), BF16),
            pltpu.VMEM((2, HALF, COLS), BF16),
            pltpu.VMEM((2, OWN, COLS), BF16),
            pltpu.VMEM((HALF, COLS), BF16),
            pltpu.VMEM((2, HALF, COLS), F32),
            pltpu.VMEM((3, NX * NY, 8, COLS), F32),
            pltpu.VMEM((3, NZ * NC, 8, COLS), F32),
        ]
        + [dma((7,)), dma((4, 2)), dma((4, 2)), dma((2, 6)), dma((2, 6)), dma((3, 22)), dma((3, 22))],
        compiler_params=pltpu.CompilerParams(
            collective_id=0, has_side_effects=True, vmem_limit_bytes=60 * 1024 * 1024
        ),
        name="iteration",
    )(
        residual, shadow, direction, old_image, solution, lower_inverse, upper_inverse,
        scal, neighbours, edge_weight, node_shift.reshape(OWN // CHUNK, CHUNK), send_rows,
    )
    new_solution, new_residual, alpha, omega, rho = outs
    return new_solution, new_residual, alpha[0], omega[0], rho[0]


def solution(mesh):
    torus = Mesh(
        mesh.devices.reshape(4, 4, 4, 2, mesh.shape["panel"]),
        ("sub_0", "sub_1", "sub_2", "sub_3", "panel"),
    )
    vec = P(SUB, "panel")
    one = P("panel")
    factor = P(SUB, None, "panel")
    in_specs = (
        vec, vec, vec, vec, vec, one, one, one, factor, factor,
        P(None, SUB), P(None, SUB), P(SUB), P(SUB, None, None),
    )
    return jax.shard_map(
        per_device, mesh=torus, in_specs=in_specs, out_specs=(vec, vec, one, one, one), check_vma=False
    )
```

```python
import functools

import jax
import jax.numpy as jnp
from jax import lax
from jax.experimental import pallas as pl
from jax.experimental.pallas import tpu as pltpu
from jax.sharding import Mesh
from jax.sharding import PartitionSpec as P

SUB = ("sub_0", "sub_1", "sub_2", "sub_3")
FLOOR_SHARE = 0.3
EPSILON = 1e-06

OWN = 1024
EXT = 1792
HALF = 896
BORDER = 384
NB = 16
COLS = 128
CHUNK = 128
NX, NY, NZ, NC = 4, 4, 4, 2
F32 = jnp.float32
BF16 = jnp.bfloat16
MESH = pl.DeviceIdType.MESH


def dot(a, b):
    return lax.dot_general(a, b, (((1,), (0,)), ((), ())), preferred_element_type=F32)


def dot_nt(a, b):
    return lax.dot_general(a, b, (((1,), (1,)), ((), ())), preferred_element_type=F32)


def chunks(body, init=0):
    def step(i, carry):
        return body(pl.ds(pl.multiple_of(i * CHUNK, CHUNK), CHUNK), carry)

    return lax.fori_loop(0, OWN // CHUNK, step, init)


def fold(x):
    return jnp.sum(x.reshape(CHUNK // 8, 8, COLS), axis=0)


def butterfly(x):
    sub = lax.broadcasted_iota(jnp.int32, x.shape, 0)
    lane = lax.broadcasted_iota(jnp.int32, x.shape, 1) // 16
    for s in (1, 2, 4):
        down = pltpu.roll(pltpu.roll(x, s, 0), 128 - 16 * s, 1)
        up = pltpu.roll(pltpu.roll(x, 8 - s, 0), 16 * s, 1)
        sub_bit = (sub // s) % 2
        lane_bit = (lane // s) % 2
        x = jnp.where(sub_bit == lane_bit, x, jnp.where(sub_bit == 1, down, up))
    return x


def kernel(
    r_hbm, s_hbm, d_hbm, oi_hbm, sol_hbm, low_hbm, up_hbm,
    rho_prev, alpha_prev, omega_prev, nbr, ew, shift, rows_ref,
    sol_out, y_out_hbm, m_out, t_out, stats,
    r, s, d, oi, sol, low, up,
    w_mat, sel, diag, code_t, base_t, wgt_t,
    xe, rq, sel_rq, g_rq, sel_u, g_u, g_v, ub, vb, y, v, m,
    x1_in, r1_in, v1_in, tail_in, p_in, u_in, y_in, p_out, u_out, y_out, inner, part, x1_c, x2_c,
    step_own, step_in, ar_a, ar_b,
    load_sem, g_send, g_recv, h_send, h_recv, p_send, p_recv, a_send, a_recv,
):
    panel = lax.axis_index("panel")
    ix, iy, iz, ic = (lax.axis_index(name) for name in SUB)
    flat = ((ix * NY + iy) * NZ + iz) * NC + ic

    def coords(index):
        return {
            "sub_0": index // (NY * NZ * NC),
            "sub_1": (index // (NZ * NC)) % NY,
            "sub_2": (index // NC) % NZ,
            "sub_3": index % NC,
        }

    total = NX * NY * NZ * NC
    above = coords((flat + 1) % total)
    below = coords((flat + total - 1) % total)
    above_one = {**above, "panel": 1}
    below_one = {**below, "panel": 1}
    partner = {"panel": 1 - panel}
    plane = [
        {"sub_0": (ix + o // NY) % NX, "sub_1": (iy + o % NY) % NY} for o in range(1, NX * NY)
    ]
    column = [
        {"sub_2": (iz + o // NC) % NZ, "sub_3": (ic + o % NC) % NC} for o in range(1, NZ * NC)
    ]

    def load(src, dst, i):
        copy = pltpu.make_async_copy(src, dst, load_sem.at[i])
        copy.start()
        return copy

    loads = [
        load(s_hbm, s, 0), load(r_hbm, r, 1), load(d_hbm, d, 2), load(oi_hbm, oi, 3),
        load(low_hbm.at[0], low, 4), load(up_hbm.at[0, pl.ds(0, OWN)], up, 5), load(sol_hbm, sol, 6),
    ]

    barrier = pltpu.get_barrier_semaphore()
    peers = plane + column + [
        above, below, {**above, "panel": 1 - panel}, {**below, "panel": 1 - panel}, partner,
    ]
    for peer in peers:
        pl.semaphore_signal(barrier, inc=1, device_id=peer, device_id_type=MESH)

    sends = []

    def remote(src, dst, ssem, rsem, peer):
        return pltpu.make_async_remote_copy(
            src_ref=src, dst_ref=dst, send_sem=ssem, recv_sem=rsem,
            device_id=peer, device_id_type=MESH,
        )

    def send(src, dst, ssem, rsem, peer):
        copy = remote(src, dst, ssem, rsem, peer)
        copy.start()
        sends.append(copy)

    def all_of(buf, n, stage, count):
        every = buf.at[n, pl.ds(0, count)]
        return remote(every, every, a_send.at[n, stage], a_recv.at[n, stage], partner)

    def reduce_start(n, rows):
        mine = ar_a.at[n, ix * NY + iy]
        mine[...] = jnp.concatenate(rows + [jnp.zeros((8 - len(rows), COLS), F32)], axis=0)
        for peer in plane:
            remote(mine, mine, a_send.at[n, 0], a_recv.at[n, 0], peer).start()
        sends.append(all_of(ar_a, n, 0, NX * NY - 1))

    def reduce_middle(n):
        all_of(ar_a, n, 0, NX * NY - 1).wait_recv()
        mine = ar_b.at[n, iz * NC + ic]
        mine[...] = jnp.sum(ar_a[n], axis=0)
        for peer in column:
            remote(mine, mine, a_send.at[n, 1], a_recv.at[n, 1], peer).start()
        sends.append(all_of(ar_b, n, 1, NZ * NC - 1))

    def reduce_end(n):
        all_of(ar_b, n, 1, NZ * NC - 1).wait_recv()
        return jnp.sum(ar_b[n], axis=0) * (1.0 / (OWN * total))

    low_rows, high_rows = pl.ds(0, BORDER), pl.ds(BORDER, BORDER)

    def ghosts_to_one(src, dst, k):
        send(src.at[low_rows], dst.at[panel, high_rows], h_send.at[k, 0], h_recv.at[k, panel, 0], below_one)
        send(src.at[high_rows], dst.at[panel, low_rows], h_send.at[k, 1], h_recv.at[k, panel, 1], above_one)

    def ghosts_at_one(dst, k, c):
        remote(dst.at[c, high_rows], dst.at[c, high_rows], h_send.at[k, 0], h_recv.at[k, c, 0], partner).wait_recv()
        remote(dst.at[c, low_rows], dst.at[c, low_rows], h_send.at[k, 1], h_recv.at[k, c, 1], partner).wait_recv()

    zero = jnp.zeros((8, COLS), F32)

    lane = lax.broadcasted_iota(jnp.int32, (CHUNK, CHUNK), 1).astype(F32)
    for n in range(2 * BORDER // CHUNK):
        side, at = n // (BORDER // CHUNK), (n % (BORDER // CHUNK)) * CHUNK
        chosen = rows_ref[0, side : side + 1, at : at + CHUNK].astype(F32)
        across = jnp.transpose(jnp.broadcast_to(chosen, (CHUNK, CHUNK)))
        for t in range(OWN // CHUNK):
            sel[n * CHUNK : (n + 1) * CHUNK, t * CHUNK : (t + 1) * CHUNK] = jnp.where(
                across == lane + float(t * CHUNK), 1.0, 0.0
            ).astype(BF16)

    loads[0].wait()
    loads[1].wait()

    def opening(at, carry):
        sr, ss = carry
        a, b = s[at, :], r[at, :]
        return sr + fold(a * b), ss + fold(a * a)

    sr, ss = chunks(opening, (zero, zero))
    pl.semaphore_wait(barrier, len(peers))
    reduce_start(0, [jnp.sum(sr, axis=0, keepdims=True), jnp.sum(ss, axis=0, keepdims=True)])

    loads[2].wait()
    loads[3].wait()
    omega_before = omega_prev[...]

    def combine(at, _):
        q = d[at, :] - omega_before * oi[at, :]
        d[at, :] = q
        rq[at, 0:COLS] = r[at, :].astype(BF16)
        rq[at, COLS : 2 * COLS] = q.astype(BF16)
        return 0

    chunks(combine)
    sel_rq[...] = dot(sel[...], rq[...]).astype(BF16)
    ghosts_to_one(sel_rq, g_rq, 0)

    def link(src, dst, n, k):
        return remote(src, dst, p_send.at[n, k], p_recv.at[n, k], partner)

    give_r1 = link(rq.at[pl.ds(0, HALF), pl.ds(0, COLS)], r1_in, 0, 7)
    give_v1 = link(vb.at[pl.ds(0, HALF)], v1_in, 1, 7)

    @pl.when(panel == 1)
    def _():
        give_r1.start()

    reduce_middle(0)

    valid = nbr[...] < EXT
    present = jnp.sum(jnp.where(valid, ew[...], 0.0), axis=0, keepdims=True)
    for t in range(OWN // CHUNK):
        at = slice(t * CHUNK, (t + 1) * CHUNK)
        line = present[:, at] + shift[t : t + 1, :]
        diag[at, :] = jnp.transpose(jnp.broadcast_to(line, (CHUNK, CHUNK)))
        for h in range(NB // 8):
            turned = butterfly(nbr[h * 8 : h * 8 + 8, at].astype(F32))
            turned = turned.astype(jnp.int32)
            inside = lax.broadcasted_iota(jnp.int32, (8, CHUNK), 1) % 16
            here = slice(h * CHUNK, (h + 1) * CHUNK)
            code_t[t * 8 : t * 8 + 8, here] = (turned // COLS) * 16 + inside
            base_t[t * 8 : t * 8 + 8, here] = turned % COLS
            wgt_t[t * 8 : t * 8 + 8, here] = butterfly(ew[h * 8 : h * 8 + 8, at])

    blocks = EXT // COLS
    code_row = lax.broadcasted_iota(jnp.int32, (blocks * 16, 2 * CHUNK), 0)
    base_row = lax.broadcasted_iota(jnp.int32, (COLS, 2 * CHUNK), 0)

    def build(g, _):
        one = pl.ds(g, 1)
        left = jnp.where(code_row == code_t[one, :], wgt_t[one, :], 0.0).astype(BF16)
        right = jnp.where(base_row == base_t[one, :], 1.0, 0.0).astype(BF16)
        found = dot_nt(left, right).astype(BF16)
        at = pl.ds(pl.multiple_of(g * 16, 16), 16)
        for a in range(blocks):
            w_mat[at, a * COLS : (a + 1) * COLS] = found[a * 16 : (a + 1) * 16, :]
        return 0

    groups = OWN // 16

    def fill(n, k):
        if n == 0:
            lax.fori_loop(k * groups // 4, (k + 1) * groups // 4, build, 0)

    q4 = HALF // 2

    def apply(n):
        tail = xe.at[n, pl.ds(HALF, OWN - HALF)]
        give_x1 = link(xe.at[n, pl.ds(0, HALF)], x1_in, n, 0)
        give_tail = link(tail, tail_in.at[n], n, 1)
        give_p0 = link(p_out.at[n, 0], p_in.at[n, 0], n, 2)
        give_p1 = link(p_out.at[n, 1], p_in.at[n, 1], n, 3)
        give_u = link(u_out.at[n], u_in.at[n], n, 4)
        give_y = link(y_out.at[n], y_in.at[n], n, 5)
        give_step = link(step_own.at[n], step_in.at[n], n, 6)

        @pl.when(panel == 0)
        def _():
            give_step.start()
            give_tail.start()

            def lower(src, dst):
                for h in range(2):
                    at = slice(h * q4, (h + 1) * q4)
                    dst[at, :] = dot(low[HALF + h * q4 : HALF + (h + 1) * q4, :], src[...]).astype(BF16)

            def upper(src, put):
                inner[0:q4, :] = dot(low[0:q4, 0:q4], src[0:q4, :]).astype(BF16)
                inner[q4:HALF, :] = dot(low[q4:HALF, :], src[...]).astype(BF16)
                put(slice(0, q4), dot(up[0:q4, :], inner[...]))
                put(slice(q4, HALF), dot(up[q4:HALF, q4:HALF], inner[q4:HALF, :]))

            x1 = xe.at[n, pl.ds(0, HALF)]
            lower(x1, p_out.at[n, 0])
            give_p0.start()

            def keep(at, value):
                y[at, :] = value

            def post(at, value):
                u_out[n, at, :] = value.astype(BF16)

            if n == 0:
                upper(x1, keep)
                fill(n, 0)
                give_x1.wait_recv()
                other = x1_in
            else:
                give_r1.wait_recv()
                give_v1.wait_recv()
                give_step.wait_recv()
                x1_c[...] = (
                    r1_in[...].astype(F32) - step_in[n, 0:1, :] * v1_in[...].astype(F32)
                ).astype(BF16)
                other = x1_c
            lower(other, p_out.at[n, 1])
            give_p1.start()
            upper(other, post)
            give_u.start()
            if n == 1:
                upper(x1, keep)
            for k in (1, 2, 3):
                fill(n, k)
            give_y.wait_recv()
            for t in range(OWN // CHUNK):
                at = slice(t * CHUNK, (t + 1) * CHUNK)
                value = y_in[n, at, :].astype(F32)
                if t < HALF // CHUNK:
                    value = value + y[at, :]
                y[at, :] = value
                ub[at, :] = value.astype(BF16)
            for copy in (give_step, give_tail, give_p0, give_p1, give_u):
                copy.wait_send()

        @pl.when(panel == 1)
        def _():
            if n == 0:
                give_x1.start()
            else:
                give_step.start()

            def extended(c, own_tail, step):
                x2_c[c, 0 : OWN - HALF, :] = own_tail
                g_r = g_rq[c, :, 0:COLS].astype(F32)
                if n == 0:
                    value = g_r + step * g_rq[c, :, COLS : 2 * COLS].astype(F32)
                else:
                    value = g_r - step * g_v[c].astype(F32)
                x2_c[c, OWN - HALF : HALF, :] = value.astype(BF16)
                part[c, 0:q4, :] = dot(low[HALF : HALF + q4, 0:q4], x2_c[c, 0:q4, :])
                part[c, q4:HALF, :] = dot(low[HALF + q4 : EXT, :], x2_c[c])

            def upper(k, put):
                inner[...] = (part[k] + p_in[n, k].astype(F32)).astype(BF16)
                for h in range(2):
                    at = slice(h * (OWN // 2), (h + 1) * (OWN // 2))
                    put(at, dot(up[at, :], inner[...]))

            received = g_rq if n == 0 else g_v
            fill(n, 0)
            ghosts_at_one(received, n, 1)
            extended(1, xe[n, HALF:OWN, :], step_own[n, 0:1, :])
            ghosts_at_one(received, n, 0)
            give_step.wait_recv()
            give_tail.wait_recv()
            extended(0, tail_in[n], step_in[n, 0:1, :])
            fill(n, 1)
            give_p0.wait_recv()

            def post(at, value):
                y_out[n, at, :] = value.astype(BF16)

            upper(0, post)
            give_y.start()
            fill(n, 2)
            give_p1.wait_recv()

            def keep(at, value):
                y[at, :] = value

            upper(1, keep)
            fill(n, 3)
            give_u.wait_recv()
            for t in range(OWN // CHUNK):
                at = slice(t * CHUNK, (t + 1) * CHUNK)
                value = y[at, :]
                if t < HALF // CHUNK:
                    value = value + u_in[n, at, :].astype(F32)
                y[at, :] = value
                ub[at, :] = value.astype(BF16)
            give_y.wait_send()
            if n == 0:
                give_x1.wait_send()
                give_r1.wait_send()
            else:
                give_step.wait_send()
                give_v1.wait_send()

    def operate(n, use):
        sel_u[n, 0:BORDER, :] = dot(sel[0:BORDER, :], ub[...]).astype(BF16)
        send(sel_u.at[n, low_rows], g_u.at[n, high_rows], g_send.at[n, 0], g_recv.at[n, 0], below)
        sel_u[n, BORDER:, :] = dot(sel[BORDER:, :], ub[...]).astype(BF16)
        send(sel_u.at[n, high_rows], g_u.at[n, low_rows], g_send.at[n, 1], g_recv.at[n, 1], above)
        copies = sends[-2:]
        v[...] = diag[...] * y[...] - dot(w_mat[:, 0:OWN], ub[...])
        for copy in copies:
            copy.wait_recv()
        for h in range(2):
            at = slice(h * (OWN // 2), (h + 1) * (OWN // 2))
            use(at, v[at, :] - dot(w_mat[at, OWN:EXT], g_u[n]))

    def whole(x):
        return jnp.sum(x, axis=0, keepdims=True)

    mean = reduce_end(0)
    rho_now, shadow_square = mean[0:1, :], mean[1:2, :]
    step_beta = rho_now / rho_prev[...] * (alpha_prev[...] / omega_before)
    step_own[0] = jnp.broadcast_to(step_beta, (8, COLS))

    def direct(at, _):
        xe[0, at, :] = (r[at, :] + step_beta * d[at, :]).astype(BF16)
        return 0

    chunks(direct)
    loads[4].wait()
    loads[5].wait()
    apply(0)

    sums = []

    def image(at, value):
        v[at, :] = value
        vb[at, :] = value.astype(BF16)
        sums.append((whole(s[at, :] * value), whole(value * value)))

    operate(0, image)
    reduce_start(1, [sums[0][i] + sums[1][i] for i in range(2)])

    @pl.when(panel == 1)
    def _():
        give_v1.start()

    sel_u[2] = dot(sel[...], vb[...]).astype(BF16)
    ghosts_to_one(sel_u.at[2], g_v, 1)
    loads[6].wait()
    reduce_middle(1)
    mean = reduce_end(1)
    denominator, image_square = mean[0:1, :], mean[1:2, :]
    step_alpha = rho_now / jnp.maximum(
        denominator, FLOOR_SHARE * jnp.sqrt(shadow_square * image_square)
    )
    step_own[1] = jnp.broadcast_to(step_alpha, (8, COLS))

    def halfway(at, carry):
        value = r[at, :] - step_alpha * v[at, :]
        m[at, :] = value
        xe[1, at, :] = value.astype(BF16)
        sol[at, :] = sol[at, :] + step_alpha * y[at, :]
        return carry + fold(s[at, :] * value)

    shadow_middle = chunks(halfway, zero)
    store = [load(sol, sol_out, 7), load(m, m_out, 8)]
    apply(1)
    store.append(load(y, y_out_hbm, 9))
    sums = []

    def test(at, value):
        v[at, :] = value
        sums.append((whole(value * m[at, :]), whole(value * value), whole(s[at, :] * value)))

    operate(1, test)
    store.append(load(v, t_out, 10))
    tm, tt, st = (sums[0][i] + sums[1][i] for i in range(3))
    reduce_start(2, [tm, tt, whole(shadow_middle), st])
    reduce_middle(2)
    mean = reduce_end(2)
    stats[...] = jnp.concatenate([mean[0:4, :], step_alpha, jnp.zeros((3, COLS), F32)], axis=0)
    for copy in store:
        copy.wait()
    for copy in sends:
        copy.wait_send()


def finish(sol, y, m, t, stats, new_sol, new_res, alpha, omega, rho):
    step_omega = stats[0:1, :] / (stats[1:2, :] + EPSILON)
    new_sol[...] = sol[...] + step_omega * y[...]
    new_res[...] = m[...] - step_omega * t[...]
    alpha[...] = stats[4:5, :]
    omega[...] = step_omega
    rho[...] = stats[2:3, :] - step_omega * stats[3:4, :]


def per_device(
    solution, residual, shadow, direction, old_image, rho_prev, alpha_prev, omega_prev,
    lower_inverse, upper_inverse, neighbours, edge_weight, node_shift, send_rows,
):
    hbm = pl.BlockSpec(memory_space=pl.ANY)
    vmem = pl.BlockSpec(memory_space=pltpu.VMEM)
    dma = pltpu.SemaphoreType.DMA

    def f32(*shape):
        return pltpu.VMEM(shape, F32)

    def b16(*shape):
        return pltpu.VMEM(shape, BF16)

    def row(x):
        return x.reshape(1, COLS)

    array = jax.ShapeDtypeStruct((OWN, COLS), F32)
    line = jax.ShapeDtypeStruct((1, COLS), F32)
    vec = f32(OWN, COLS)
    tables = [pltpu.VMEM((OWN // 16, 256), kind) for kind in (jnp.int32, jnp.int32, F32)]
    parts = pl.pallas_call(
        kernel,
        out_shape=[array] * 4 + [jax.ShapeDtypeStruct((8, COLS), F32)],
        in_specs=[hbm] * 7 + [vmem] * 7,
        out_specs=[hbm] * 4 + [vmem],
        scratch_shapes=[vec] * 5
        + [b16(EXT, HALF), b16(OWN, HALF)]
        + [b16(OWN, EXT), b16(2 * BORDER, OWN), vec] + tables
        + [
            b16(2, OWN, COLS), b16(OWN, 2 * COLS), b16(2 * BORDER, 2 * COLS),
            b16(2, 2 * BORDER, 2 * COLS), b16(3, 2 * BORDER, COLS), b16(2, 2 * BORDER, COLS),
            b16(2, 2 * BORDER, COLS), b16(OWN, COLS), b16(OWN, COLS), vec, vec, vec,
        ]
        + [
            b16(HALF, COLS), b16(HALF, COLS), b16(HALF, COLS), b16(2, OWN - HALF, COLS),
            b16(2, 2, HALF, COLS), b16(2, HALF, COLS), b16(2, OWN, COLS),
            b16(2, 2, HALF, COLS), b16(2, HALF, COLS), b16(2, OWN, COLS),
            b16(HALF, COLS), f32(2, HALF, COLS), b16(HALF, COLS), b16(2, HALF, COLS),
        ]
        + [f32(2, 8, COLS), f32(2, 8, COLS), f32(3, NX * NY, 8, COLS), f32(3, NZ * NC, 8, COLS)]
        + [
            dma((11,)), dma((2, 2)), dma((2, 2)), dma((2, 2)), dma((2, 2, 2)),
            dma((2, 8)), dma((2, 8)), dma((3, 2)), dma((3, 2)),
        ],
        compiler_params=pltpu.CompilerParams(
            collective_id=0, has_side_effects=True, vmem_limit_bytes=60 * 1024 * 1024
        ),
        name="iteration",
    )(
        residual, shadow, direction, old_image, solution, lower_inverse, upper_inverse,
        row(rho_prev), row(alpha_prev), row(omega_prev),
        neighbours, edge_weight, node_shift.reshape(OWN // CHUNK, CHUNK), send_rows,
    )
    steps = 4
    block = pl.BlockSpec((OWN // steps, COLS), lambda i: (i, 0))
    fixed = pl.BlockSpec((1, COLS), lambda i: (0, 0))
    new_solution, new_residual, alpha, omega, rho = pl.pallas_call(
        finish,
        out_shape=[array] * 2 + [line] * 3,
        grid=(steps,),
        in_specs=[block] * 4 + [pl.BlockSpec((8, COLS), lambda i: (0, 0))],
        out_specs=[block] * 2 + [fixed] * 3,
        name="finish",
    )(*parts)
    return new_solution, new_residual, alpha[0], omega[0], rho[0]


def solution(mesh):
    torus = Mesh(
        mesh.devices.reshape(4, 4, 4, 2, mesh.shape["panel"]),
        ("sub_0", "sub_1", "sub_2", "sub_3", "panel"),
    )
    vec = P(SUB, "panel")
    one = P("panel")
    factor = P(SUB, None, "panel")
    in_specs = (
        vec, vec, vec, vec, vec, one, one, one, factor, factor,
        P(None, SUB), P(None, SUB), P(SUB), P(SUB, None, None),
    )
    return jax.shard_map(
        per_device, mesh=torus, in_specs=in_specs, out_specs=(vec, vec, one, one, one), check_vma=False
    )
```

```python
import functools

import jax
import jax.numpy as jnp
from jax import lax
from jax.experimental import pallas as pl
from jax.experimental.pallas import tpu as pltpu
from jax.sharding import Mesh
from jax.sharding import PartitionSpec as P

SUB = ("sub_0", "sub_1", "sub_2", "sub_3")
FLOOR_SHARE = 0.3
EPSILON = 1e-06

OWN = 1024
EXT = 1792
HALF = 896
BORDER = 384
NB = 16
COLS = 128
CHUNK = 128
NX, NY, NZ, NC = 4, 4, 4, 2
F32 = jnp.float32
BF16 = jnp.bfloat16
MESH = pl.DeviceIdType.MESH


def dot(a, b):
    return lax.dot_general(a, b, (((1,), (0,)), ((), ())), preferred_element_type=F32)


def dot_nt(a, b):
    return lax.dot_general(a, b, (((1,), (1,)), ((), ())), preferred_element_type=F32)


def chunks(body, init=0):
    def step(i, carry):
        return body(pl.ds(pl.multiple_of(i * CHUNK, CHUNK), CHUNK), carry)

    return lax.fori_loop(0, OWN // CHUNK, step, init, unroll=True)


def fold(x):
    return jnp.sum(x.reshape(CHUNK // 8, 8, COLS), axis=0)


def butterfly(x):
    sub = lax.broadcasted_iota(jnp.int32, x.shape, 0)
    lane = lax.broadcasted_iota(jnp.int32, x.shape, 1) // 16
    for s in (1, 2, 4):
        down = pltpu.roll(pltpu.roll(x, s, 0), 128 - 16 * s, 1)
        up = pltpu.roll(pltpu.roll(x, 8 - s, 0), 16 * s, 1)
        sub_bit = (sub // s) % 2
        lane_bit = (lane // s) % 2
        x = jnp.where(sub_bit == lane_bit, x, jnp.where(sub_bit == 1, down, up))
    return x


def kernel(
    r_hbm, s_hbm, d_hbm, oi_hbm, sol_hbm, low_hbm, up_hbm,
    rho_prev, alpha_prev, omega_prev, nbr, ew, shift, rows_ref,
    sol_out, y_out_hbm, m_out, t_out, stats,
    r, s, d, oi, sol, low, up,
    w_mat, sel, diag, code_t, base_t, wgt_t,
    xe, rb, qb, sel_r, g_r, g_q, sel_u, g_u, g_v, ub, vb, y_first, y_second, v, m,
    x1_in, r1_in, v1_in, tail_in, p_in, u_in, y_in, p_out, u_out, y_out, inner, part, x1_c, x2_c,
    step_own, step_in, middle_sum, red_a0, red_b0, red_a1, red_b1, red_a2, red_b2,
    load_sem, g_send, g_recv, h_send, h_recv, p_send, p_recv, a_send, a_recv,
):
    panel = lax.axis_index("panel")
    ix, iy, iz, ic = (lax.axis_index(name) for name in SUB)
    flat = ((ix * NY + iy) * NZ + iz) * NC + ic

    def coords(index):
        return {
            "sub_0": index // (NY * NZ * NC),
            "sub_1": (index // (NZ * NC)) % NY,
            "sub_2": (index // NC) % NZ,
            "sub_3": index % NC,
        }

    total = NX * NY * NZ * NC
    above = coords((flat + 1) % total)
    below = coords((flat + total - 1) % total)
    above_one = {**above, "panel": 1}
    below_one = {**below, "panel": 1}
    partner = {"panel": 1 - panel}
    plane = [
        {"sub_0": (ix + o // NY) % NX, "sub_1": (iy + o % NY) % NY} for o in range(1, NX * NY)
    ]
    column = [
        {"sub_2": (iz + o // NC) % NZ, "sub_3": (ic + o % NC) % NC} for o in range(1, NZ * NC)
    ]

    def load(src, dst, i):
        copy = pltpu.make_async_copy(src, dst, load_sem.at[i])
        copy.start()
        return copy

    loads = [
        load(s_hbm, s, 0), load(r_hbm, r, 1), load(d_hbm, d, 2), load(oi_hbm, oi, 3),
    ]

    barrier = pltpu.get_barrier_semaphore()
    peers = plane + column + [
        above, below, {**above, "panel": 1 - panel}, {**below, "panel": 1 - panel}, partner,
    ]
    for peer in peers:
        pl.semaphore_signal(barrier, inc=1, device_id=peer, device_id_type=MESH)

    sends = []

    def remote(src, dst, ssem, rsem, peer):
        return pltpu.make_async_remote_copy(
            src_ref=src, dst_ref=dst, send_sem=ssem, recv_sem=rsem,
            device_id=peer, device_id_type=MESH,
        )

    def send(src, dst, ssem, rsem, peer):
        copy = remote(src, dst, ssem, rsem, peer)
        copy.start()
        sends.append(copy)

    red_a, red_b = (red_a0, red_a1, red_a2), (red_b0, red_b1, red_b2)

    def all_of(buf, n, stage, count):
        every = buf.at[pl.ds(0, count)]
        return remote(every, every, a_send.at[n, stage], a_recv.at[n, stage], partner)

    def reduce_start(n, rows):
        mine = red_a[n].at[ix * NY + iy]
        mine[...] = jnp.concatenate(rows, axis=0)
        for peer in plane:
            remote(mine, mine, a_send.at[n, 0], a_recv.at[n, 0], peer).start()
        sends.append(all_of(red_a[n], n, 0, NX * NY - 1))

    def reduce_middle(n):
        all_of(red_a[n], n, 0, NX * NY - 1).wait_recv()
        mine = red_b[n].at[iz * NC + ic]
        mine[...] = jnp.sum(red_a[n][...], axis=0)
        for peer in column:
            remote(mine, mine, a_send.at[n, 1], a_recv.at[n, 1], peer).start()
        sends.append(all_of(red_b[n], n, 1, NZ * NC - 1))

    def reduce_end(n):
        all_of(red_b[n], n, 1, NZ * NC - 1).wait_recv()
        return jnp.sum(red_b[n][...], axis=0) * (1.0 / (OWN * total))

    low_rows, high_rows = pl.ds(0, BORDER), pl.ds(BORDER, BORDER)

    def ghosts_to_one(src, dst, k):
        send(src.at[low_rows], dst.at[panel, high_rows], h_send.at[k, 0], h_recv.at[k, panel, 0], below_one)
        send(src.at[high_rows], dst.at[panel, low_rows], h_send.at[k, 1], h_recv.at[k, panel, 1], above_one)

    def ghosts_at_one(dst, k, c):
        remote(dst.at[c, high_rows], dst.at[c, high_rows], h_send.at[k, 0], h_recv.at[k, c, 0], partner).wait_recv()
        remote(dst.at[c, low_rows], dst.at[c, low_rows], h_send.at[k, 1], h_recv.at[k, c, 1], partner).wait_recv()

    zero = jnp.zeros((8, COLS), F32)

    lane = lax.broadcasted_iota(jnp.int32, (CHUNK, CHUNK), 1).astype(F32)
    for n in range(2 * BORDER // CHUNK):
        side, at = n // (BORDER // CHUNK), (n % (BORDER // CHUNK)) * CHUNK
        chosen = rows_ref[0, side : side + 1, at : at + CHUNK].astype(F32)
        across = jnp.transpose(jnp.broadcast_to(chosen, (CHUNK, CHUNK)))
        for t in range(OWN // CHUNK):
            sel[n * CHUNK : (n + 1) * CHUNK, t * CHUNK : (t + 1) * CHUNK] = jnp.where(
                across == lane + float(t * CHUNK), 1.0, 0.0
            ).astype(BF16)

    loads[0].wait()
    loads[1].wait()
    loads.extend([
        load(low_hbm.at[0], low, 4), load(up_hbm.at[0, pl.ds(0, OWN)], up, 5), load(sol_hbm, sol, 6),
    ])

    def opening(at, carry):
        sr, ss = carry
        a, b = s[at, :], r[at, :]
        rb[at, :] = b.astype(BF16)
        return sr + fold(a * b), ss + fold(a * a)

    sr, ss = chunks(opening, (zero, zero))
    sel_r[0] = dot(sel[...], rb[...]).astype(BF16)
    pl.semaphore_wait(barrier, len(peers))
    reduce_start(0, [jnp.sum(sr, axis=0, keepdims=True), jnp.sum(ss, axis=0, keepdims=True)])
    ghosts_to_one(sel_r.at[0], g_r, 2)

    loads[2].wait()
    loads[3].wait()
    omega_before = omega_prev[...]

    def combine(at, _):
        q = d[at, :] - omega_before * oi[at, :]
        d[at, :] = q
        qb[at, :] = q.astype(BF16)
        return 0

    chunks(combine)
    sel_r[1] = dot(sel[...], qb[...]).astype(BF16)
    ghosts_to_one(sel_r.at[1], g_q, 0)

    def link(src, dst, n, k):
        return remote(src, dst, p_send.at[n, k], p_recv.at[n, k], partner)

    give_r1 = link(rb.at[pl.ds(0, HALF)], r1_in, 0, 7)
    give_v1 = link(vb.at[pl.ds(0, HALF)], v1_in, 1, 7)

    reduce_middle(0)

    valid = nbr[...] < EXT
    present = jnp.sum(jnp.where(valid, ew[...], 0.0), axis=0, keepdims=True)
    for t in range(OWN // CHUNK):
        at = slice(t * CHUNK, (t + 1) * CHUNK)
        line = present[:, at] + shift[t : t + 1, :]
        diag[at, :] = jnp.transpose(jnp.broadcast_to(line, (CHUNK, CHUNK)))
        for h in range(NB // 8):
            turned = butterfly(nbr[h * 8 : h * 8 + 8, at].astype(F32))
            turned = turned.astype(jnp.int32)
            inside = lax.broadcasted_iota(jnp.int32, (8, CHUNK), 1) % 16
            here = slice(h * CHUNK, (h + 1) * CHUNK)
            code_t[t * 8 : t * 8 + 8, here] = (turned // COLS) * 16 + inside
            base_t[t * 8 : t * 8 + 8, here] = turned % COLS
            wgt_t[t * 8 : t * 8 + 8, here] = butterfly(ew[h * 8 : h * 8 + 8, at])

    blocks = EXT // COLS
    code_row = lax.broadcasted_iota(jnp.int32, (blocks * 16, 2 * CHUNK), 0)
    base_row = lax.broadcasted_iota(jnp.int32, (COLS, 2 * CHUNK), 0)

    def build(g, _):
        one = pl.ds(g, 1)
        left = jnp.where(code_row == code_t[one, :], wgt_t[one, :], 0.0).astype(BF16)
        right = jnp.where(base_row == base_t[one, :], 1.0, 0.0).astype(BF16)
        found = dot_nt(left, right).astype(BF16)
        at = pl.ds(pl.multiple_of(g * 16, 16), 16)
        for a in range(blocks):
            w_mat[at, a * COLS : (a + 1) * COLS] = found[a * 16 : (a + 1) * 16, :]
        return 0

    groups = OWN // 16

    def fill(n, k):
        if n == 0:
            lax.fori_loop(k * groups // 4, (k + 1) * groups // 4, build, 0)
        elif k == 1:
            step_alpha = step_own[1, 0:1, :]

            def halfway(at, carry):
                value = r[at, :] - step_alpha * v[at, :]
                m[at, :] = value
                sol[at, :] = sol[at, :] + step_alpha * y_first[at, :]
                return carry + fold(s[at, :] * value)

            middle_sum[...] = chunks(halfway, zero)

    q4 = HALF // 2

    def apply(n, y):
        tail = xe.at[n, pl.ds(HALF, OWN - HALF)]
        if n == 0:
            give_x1 = link(xe.at[n, pl.ds(0, HALF)], x1_in, n, 0)
        give_tail = link(tail, tail_in.at[n], n, 1)
        give_p0 = link(p_out.at[n, 0], p_in.at[n, 0], n, 2)
        give_p1 = link(p_out.at[n, 1], p_in.at[n, 1], n, 3)
        give_u = link(u_out.at[n], u_in.at[n], n, 4)
        give_y = link(y_out.at[n], y_in.at[n], n, 5)
        give_step = link(step_own.at[n], step_in.at[n], n, 6)

        @pl.when(panel == 0)
        def _():
            give_step.start()
            give_tail.start()

            def lower(src, dst):
                for h in range(2):
                    at = slice(h * q4, (h + 1) * q4)
                    dst[at, :] = dot(low[HALF + h * q4 : HALF + (h + 1) * q4, :], src[...]).astype(BF16)

            def upper(src, put):
                inner[0:q4, :] = dot(low[0:q4, 0:q4], src[0:q4, :]).astype(BF16)
                inner[q4:HALF, :] = dot(low[q4:HALF, :], src[...]).astype(BF16)
                put(slice(0, q4), dot(up[0:q4, :], inner[...]))
                put(slice(q4, HALF), dot(up[q4:HALF, q4:HALF], inner[q4:HALF, :]))

            x1 = xe.at[n, pl.ds(0, HALF)]
            lower(x1, p_out.at[n, 0])
            give_p0.start()

            def keep(at, value):
                y[at, :] = value

            def post(at, value):
                u_out[n, at, :] = value.astype(BF16)

            if n == 0:
                upper(x1, keep)
                fill(n, 0)
                give_x1.wait_recv()
                other = x1_in
            else:
                give_r1.wait_recv()
                give_v1.wait_recv()
                give_step.wait_recv()
                x1_c[...] = (
                    r1_in[...].astype(F32) - step_in[n, 0:1, :] * v1_in[...].astype(F32)
                ).astype(BF16)
                other = x1_c
            lower(other, p_out.at[n, 1])
            give_p1.start()
            upper(other, post)
            give_u.start()
            if n == 1:
                upper(x1, keep)
            for k in (1, 2, 3):
                fill(n, k)
            give_y.wait_recv()
            for t in range(OWN // CHUNK):
                at = slice(t * CHUNK, (t + 1) * CHUNK)
                value = y_in[n, at, :].astype(F32)
                if t < HALF // CHUNK:
                    value = value + y[at, :]
                y[at, :] = value
                ub[at, :] = value.astype(BF16)
            for copy in (give_step, give_tail, give_p0, give_p1, give_u):
                copy.wait_send()

        @pl.when(panel == 1)
        def _():
            if n == 0:
                give_x1.start()
                give_r1.start()
            else:
                give_step.start()

            def extended(c, own_tail, step):
                x2_c[c, 0 : OWN - HALF, :] = own_tail
                if n == 0:
                    value = g_r[c].astype(F32) + step * g_q[c].astype(F32)
                else:
                    value = g_r[c].astype(F32) - step * g_v[c].astype(F32)
                x2_c[c, OWN - HALF : HALF, :] = value.astype(BF16)
                part[c, 0:q4, :] = dot(low[HALF : HALF + q4, 0:q4], x2_c[c, 0:q4, :])
                part[c, q4:HALF, :] = dot(low[HALF + q4 : EXT, :], x2_c[c])

            def upper(k, put):
                inner[...] = (part[k] + p_in[n, k].astype(F32)).astype(BF16)
                for h in range(2):
                    at = slice(h * (OWN // 2), (h + 1) * (OWN // 2))
                    put(at, dot(up[at, :], inner[...]))

            received = g_q if n == 0 else g_v
            fill(n, 0)
            if n == 0:
                ghosts_at_one(g_r, 2, 1)
            ghosts_at_one(received, n, 1)
            extended(1, xe[n, HALF:OWN, :], step_own[n, 0:1, :])
            if n == 0:
                ghosts_at_one(g_r, 2, 0)
            ghosts_at_one(received, n, 0)
            give_step.wait_recv()
            give_tail.wait_recv()
            extended(0, tail_in[n], step_in[n, 0:1, :])
            fill(n, 1)
            give_p0.wait_recv()

            def post(at, value):
                y_out[n, at, :] = value.astype(BF16)

            upper(0, post)
            give_y.start()
            fill(n, 2)
            give_p1.wait_recv()

            def keep(at, value):
                y[at, :] = value

            upper(1, keep)
            fill(n, 3)
            give_u.wait_recv()
            for t in range(OWN // CHUNK):
                at = slice(t * CHUNK, (t + 1) * CHUNK)
                value = y[at, :]
                if t < HALF // CHUNK:
                    value = value + u_in[n, at, :].astype(F32)
                y[at, :] = value
                ub[at, :] = value.astype(BF16)
            give_y.wait_send()
            if n == 0:
                give_x1.wait_send()
                give_r1.wait_send()
            else:
                give_step.wait_send()
                give_v1.wait_send()

    def operate(n, y, use):
        sel_u[n, 0:BORDER, :] = dot(sel[0:BORDER, :], ub[...]).astype(BF16)
        send(sel_u.at[n, low_rows], g_u.at[n, high_rows], g_send.at[n, 0], g_recv.at[n, 0], below)
        sel_u[n, BORDER:, :] = dot(sel[BORDER:, :], ub[...]).astype(BF16)
        send(sel_u.at[n, high_rows], g_u.at[n, low_rows], g_send.at[n, 1], g_recv.at[n, 1], above)
        copies = sends[-2:]
        v[...] = diag[...] * y[...] - dot(w_mat[:, 0:OWN], ub[...])
        for copy in copies:
            copy.wait_recv()
        for h in range(2):
            at = slice(h * (OWN // 2), (h + 1) * (OWN // 2))
            use(at, v[at, :] - dot(w_mat[at, OWN:EXT], g_u[n]))

    def whole(x):
        return jnp.sum(x, axis=0, keepdims=True)

    mean = reduce_end(0)
    rho_now, shadow_square = mean[0:1, :], mean[1:2, :]
    step_beta = rho_now / rho_prev[...] * (alpha_prev[...] / omega_before)
    step_own[0] = jnp.broadcast_to(step_beta, (8, COLS))

    def direct(at, _):
        xe[0, at, :] = (r[at, :] + step_beta * d[at, :]).astype(BF16)
        return 0

    chunks(direct)
    loads[4].wait()
    loads[5].wait()
    apply(0, y_first)

    sums = []

    def image(at, value):
        v[at, :] = value
        vb[at, :] = value.astype(BF16)
        sums.append((whole(s[at, :] * value), whole(value * value)))

    operate(0, y_first, image)
    reduce_start(1, [sums[0][i] + sums[1][i] for i in range(2)])

    @pl.when(panel == 1)
    def _():
        give_v1.start()

    sel_u[2] = dot(sel[...], vb[...]).astype(BF16)
    ghosts_to_one(sel_u.at[2], g_v, 1)
    loads[6].wait()
    reduce_middle(1)
    mean = reduce_end(1)
    denominator, image_square = mean[0:1, :], mean[1:2, :]
    step_alpha = rho_now / jnp.maximum(
        denominator, FLOOR_SHARE * jnp.sqrt(shadow_square * image_square)
    )
    step_own[1] = jnp.broadcast_to(step_alpha, (8, COLS))

    def middle(at, _):
        xe[1, at, :] = (r[at, :] - step_alpha * v[at, :]).astype(BF16)
        return 0

    chunks(middle)
    apply(1, y_second)
    store = [load(sol, sol_out, 7), load(m, m_out, 8), load(y_second, y_out_hbm, 9)]
    sums = []

    def test(at, value):
        v[at, :] = value
        sums.append((whole(value * m[at, :]), whole(value * value), whole(s[at, :] * value)))

    operate(1, y_second, test)
    store.append(load(v, t_out, 10))
    tm, tt, st = (sums[0][i] + sums[1][i] for i in range(3))
    reduce_start(2, [tm, tt, whole(middle_sum[...]), st])
    reduce_middle(2)
    mean = reduce_end(2)
    stats[...] = jnp.concatenate([mean[0:4, :], step_alpha, jnp.zeros((3, COLS), F32)], axis=0)
    for copy in store:
        copy.wait()
    for copy in sends:
        copy.wait_send()


def finish(sol, y, m, t, stats, new_sol, new_res, alpha, omega, rho):
    step_omega = stats[0:1, :] / (stats[1:2, :] + EPSILON)
    new_sol[...] = sol[...] + step_omega * y[...]
    new_res[...] = m[...] - step_omega * t[...]
    alpha[...] = stats[4:5, :]
    omega[...] = step_omega
    rho[...] = stats[2:3, :] - step_omega * stats[3:4, :]


def per_device(
    solution, residual, shadow, direction, old_image, rho_prev, alpha_prev, omega_prev,
    lower_inverse, upper_inverse, neighbours, edge_weight, node_shift, send_rows,
):
    hbm = pl.BlockSpec(memory_space=pl.ANY)
    vmem = pl.BlockSpec(memory_space=pltpu.VMEM)
    dma = pltpu.SemaphoreType.DMA

    def f32(*shape):
        return pltpu.VMEM(shape, F32)

    def b16(*shape):
        return pltpu.VMEM(shape, BF16)

    def row(x):
        return x.reshape(1, COLS)

    array = jax.ShapeDtypeStruct((OWN, COLS), F32)
    line = jax.ShapeDtypeStruct((1, COLS), F32)
    vec = f32(OWN, COLS)
    tables = [pltpu.VMEM((OWN // 16, 256), kind) for kind in (jnp.int32, jnp.int32, F32)]
    parts = pl.pallas_call(
        kernel,
        out_shape=[array] * 4 + [jax.ShapeDtypeStruct((8, COLS), F32)],
        in_specs=[hbm] * 7 + [vmem] * 7,
        out_specs=[hbm] * 4 + [vmem],
        scratch_shapes=[vec] * 5
        + [b16(EXT, HALF), b16(OWN, HALF)]
        + [b16(OWN, EXT), b16(2 * BORDER, OWN), vec] + tables
        + [
            b16(2, OWN, COLS), b16(OWN, COLS), b16(OWN, COLS), b16(2, 2 * BORDER, COLS),
            b16(2, 2 * BORDER, COLS), b16(2, 2 * BORDER, COLS), b16(3, 2 * BORDER, COLS), b16(2, 2 * BORDER, COLS),
            b16(2, 2 * BORDER, COLS), b16(OWN, COLS), b16(OWN, COLS), vec, vec, vec, vec,
        ]
        + [
            b16(HALF, COLS), b16(HALF, COLS), b16(HALF, COLS), b16(2, OWN - HALF, COLS),
            b16(2, 2, HALF, COLS), b16(2, HALF, COLS), b16(2, OWN, COLS),
            b16(2, 2, HALF, COLS), b16(2, HALF, COLS), b16(2, OWN, COLS),
            b16(HALF, COLS), f32(2, HALF, COLS), b16(HALF, COLS), b16(2, HALF, COLS),
        ]
        + [f32(2, 8, COLS), f32(2, 8, COLS), f32(8, COLS)]
        + [f32(k, rows, COLS) for rows in (2, 2, 4) for k in (NX * NY, NZ * NC)]
        + [
            dma((11,)), dma((2, 2)), dma((2, 2)), dma((3, 2)), dma((3, 2, 2)),
            dma((2, 8)), dma((2, 8)), dma((3, 2)), dma((3, 2)),
        ],
        compiler_params=pltpu.CompilerParams(
            collective_id=0, has_side_effects=True, vmem_limit_bytes=60 * 1024 * 1024
        ),
        name="iteration",
    )(
        residual, shadow, direction, old_image, solution, lower_inverse, upper_inverse,
        row(rho_prev), row(alpha_prev), row(omega_prev),
        neighbours, edge_weight, node_shift.reshape(OWN // CHUNK, CHUNK), send_rows,
    )
    steps = 1
    block = pl.BlockSpec((OWN // steps, COLS), lambda i: (i, 0))
    fixed = pl.BlockSpec((1, COLS), lambda i: (0, 0))
    new_solution, new_residual, alpha, omega, rho = pl.pallas_call(
        finish,
        out_shape=[array] * 2 + [line] * 3,
        grid=(steps,),
        in_specs=[block] * 4 + [pl.BlockSpec((8, COLS), lambda i: (0, 0))],
        out_specs=[block] * 2 + [fixed] * 3,
        name="finish",
    )(*parts)
    return new_solution, new_residual, alpha[0], omega[0], rho[0]


def solution(mesh):
    torus = Mesh(
        mesh.devices.reshape(4, 4, 4, 2, mesh.shape["panel"]),
        ("sub_0", "sub_1", "sub_2", "sub_3", "panel"),
    )
    vec = P(SUB, "panel")
    one = P("panel")
    factor = P(SUB, None, "panel")
    in_specs = (
        vec, vec, vec, vec, vec, one, one, one, factor, factor,
        P(None, SUB), P(None, SUB), P(SUB), P(SUB, None, None),
    )
    return jax.shard_map(
        per_device, mesh=torus, in_specs=in_specs, out_specs=(vec, vec, one, one, one), check_vma=False
    )
```

```python
import functools

import jax
import jax.numpy as jnp
from jax import lax
from jax.experimental import pallas as pl
from jax.experimental.pallas import tpu as pltpu
from jax.sharding import Mesh
from jax.sharding import PartitionSpec as P

SUB = ("sub_0", "sub_1", "sub_2", "sub_3")
FLOOR_SHARE = 0.3
EPSILON = 1e-06

OWN = 1024
EXT = 1792
HALF = 896
BORDER = 384
NB = 16
COLS = 128
CHUNK = 128
NX, NY, NZ, NC = 4, 4, 4, 2
F32 = jnp.float32
BF16 = jnp.bfloat16
MESH = pl.DeviceIdType.MESH


def dot(a, b):
    return lax.dot_general(a, b, (((1,), (0,)), ((), ())), preferred_element_type=F32)


def dot_nt(a, b):
    return lax.dot_general(a, b, (((1,), (1,)), ((), ())), preferred_element_type=F32)


def chunks(body, init=0):
    def step(i, carry):
        return body(pl.ds(pl.multiple_of(i * CHUNK, CHUNK), CHUNK), carry)

    return lax.fori_loop(0, OWN // CHUNK, step, init, unroll=True)


def fold(x):
    return jnp.sum(x.reshape(CHUNK // 8, 8, COLS), axis=0)


def butterfly(x):
    sub = lax.broadcasted_iota(jnp.int32, x.shape, 0)
    lane = lax.broadcasted_iota(jnp.int32, x.shape, 1) // 16
    for s in (1, 2, 4):
        down = pltpu.roll(pltpu.roll(x, s, 0), 128 - 16 * s, 1)
        up = pltpu.roll(pltpu.roll(x, 8 - s, 0), 16 * s, 1)
        sub_bit = (sub // s) % 2
        lane_bit = (lane // s) % 2
        x = jnp.where(sub_bit == lane_bit, x, jnp.where(sub_bit == 1, down, up))
    return x


def kernel(
    r_hbm, s_hbm, d_hbm, oi_hbm, sol_hbm, low_hbm, up_hbm,
    rho_prev, alpha_prev, omega_prev, nbr, ew, shift, rows_ref,
    sol_out, y_out_hbm, m_out, t_out, stats,
    r, s, d, oi, sol, low, up,
    w_mat, sel, diag, code_t, base_t, wgt_t,
    xe, rb, qb, sel_r, g_r, g_q, sel_u, g_u, g_v, ub, vb, y_first, y_second, v, m,
    x1_in, r1_in, v1_in, tail_in, p_in, u_in, y_in, p_out, u_out, y_out, inner, part, x1_c, x2_c,
    step_own, step_in, middle_sum, red_a0, red_b0, red_a1, red_b1, red_a2, red_b2,
    load_sem, g_send, g_recv, h_send, h_recv, p_send, p_recv, a_send, a_recv,
):
    panel = lax.axis_index("panel")
    ix, iy, iz, ic = (lax.axis_index(name) for name in SUB)
    flat = ((ix * NY + iy) * NZ + iz) * NC + ic

    def coords(index):
        return {
            "sub_0": index // (NY * NZ * NC),
            "sub_1": (index // (NZ * NC)) % NY,
            "sub_2": (index // NC) % NZ,
            "sub_3": index % NC,
        }

    total = NX * NY * NZ * NC
    above = coords((flat + 1) % total)
    below = coords((flat + total - 1) % total)
    far_peer = coords((flat + total + 2 * ic - 1) % total)
    near_peer = coords((flat + total + 1 - 2 * ic) % total)
    above_one = {**above, "panel": 1}
    below_one = {**below, "panel": 1}
    partner = {"panel": 1 - panel}
    plane = [
        {"sub_0": (ix + o // NY) % NX, "sub_1": (iy + o % NY) % NY} for o in range(1, NX * NY)
    ]
    column = [
        {"sub_2": (iz + o // NC) % NZ, "sub_3": (ic + o % NC) % NC} for o in range(1, NZ * NC)
    ]

    def load(src, dst, i):
        copy = pltpu.make_async_copy(src, dst, load_sem.at[i])
        copy.start()
        return copy

    loads = [
        load(s_hbm, s, 0), load(r_hbm, r, 1), load(d_hbm, d, 2), load(oi_hbm, oi, 3),
    ]

    barrier = pltpu.get_barrier_semaphore()
    peers = plane + column + [
        above, below, {**above, "panel": 1 - panel}, {**below, "panel": 1 - panel}, partner,
    ]
    for peer in peers:
        pl.semaphore_signal(barrier, inc=1, device_id=peer, device_id_type=MESH)

    sends = []

    def remote(src, dst, ssem, rsem, peer):
        return pltpu.make_async_remote_copy(
            src_ref=src, dst_ref=dst, send_sem=ssem, recv_sem=rsem,
            device_id=peer, device_id_type=MESH,
        )

    def send(src, dst, ssem, rsem, peer):
        copy = remote(src, dst, ssem, rsem, peer)
        copy.start()
        sends.append(copy)

    red_a, red_b = (red_a0, red_a1, red_a2), (red_b0, red_b1, red_b2)

    def all_of(buf, n, stage, count):
        every = buf.at[pl.ds(0, count)]
        return remote(every, every, a_send.at[n, stage], a_recv.at[n, stage], partner)

    def reduce_start(n, rows):
        mine = red_a[n].at[ix * NY + iy]
        mine[...] = jnp.concatenate(rows, axis=0)
        for peer in plane:
            remote(mine, mine, a_send.at[n, 0], a_recv.at[n, 0], peer).start()
        sends.append(all_of(red_a[n], n, 0, NX * NY - 1))

    def reduce_middle(n):
        all_of(red_a[n], n, 0, NX * NY - 1).wait_recv()
        mine = red_b[n].at[iz * NC + ic]
        mine[...] = jnp.sum(red_a[n][...], axis=0)
        for peer in column:
            remote(mine, mine, a_send.at[n, 1], a_recv.at[n, 1], peer).start()
        sends.append(all_of(red_b[n], n, 1, NZ * NC - 1))

    def reduce_end(n):
        all_of(red_b[n], n, 1, NZ * NC - 1).wait_recv()
        return jnp.sum(red_b[n][...], axis=0) * (1.0 / (OWN * total))

    low_rows, high_rows = pl.ds(0, BORDER), pl.ds(BORDER, BORDER)

    def ghosts_to_one(src, dst, k):
        send(src.at[low_rows], dst.at[panel, high_rows], h_send.at[k, 0], h_recv.at[k, panel, 0], below_one)
        send(src.at[high_rows], dst.at[panel, low_rows], h_send.at[k, 1], h_recv.at[k, panel, 1], above_one)

    def ghosts_at_one(dst, k, c):
        remote(dst.at[c, high_rows], dst.at[c, high_rows], h_send.at[k, 0], h_recv.at[k, c, 0], partner).wait_recv()
        remote(dst.at[c, low_rows], dst.at[c, low_rows], h_send.at[k, 1], h_recv.at[k, c, 1], partner).wait_recv()

    zero = jnp.zeros((8, COLS), F32)

    lane = lax.broadcasted_iota(jnp.int32, (CHUNK, CHUNK), 1).astype(F32)
    for n in range(2 * BORDER // CHUNK):
        side, at = n // (BORDER // CHUNK), (n % (BORDER // CHUNK)) * CHUNK
        chosen = rows_ref[0, side : side + 1, at : at + CHUNK].astype(F32)
        across = jnp.transpose(jnp.broadcast_to(chosen, (CHUNK, CHUNK)))
        for t in range(OWN // CHUNK):
            sel[n * CHUNK : (n + 1) * CHUNK, t * CHUNK : (t + 1) * CHUNK] = jnp.where(
                across == lane + float(t * CHUNK), 1.0, 0.0
            ).astype(BF16)

    loads[0].wait()
    loads[1].wait()
    loads.extend([
        load(low_hbm.at[0], low, 4), load(up_hbm.at[0, pl.ds(0, OWN)], up, 5), load(sol_hbm, sol, 6),
    ])

    def opening(at, carry):
        sr, ss = carry
        a, b = s[at, :], r[at, :]
        rb[at, :] = b.astype(BF16)
        return sr + fold(a * b), ss + fold(a * a)

    sr, ss = chunks(opening, (zero, zero))
    sel_r[0] = dot(sel[...], rb[...]).astype(BF16)
    pl.semaphore_wait(barrier, len(peers))
    reduce_start(0, [jnp.sum(sr, axis=0, keepdims=True), jnp.sum(ss, axis=0, keepdims=True)])
    ghosts_to_one(sel_r.at[0], g_r, 2)

    loads[2].wait()
    loads[3].wait()
    omega_before = omega_prev[...]

    def combine(at, _):
        q = d[at, :] - omega_before * oi[at, :]
        d[at, :] = q
        qb[at, :] = q.astype(BF16)
        return 0

    chunks(combine)
    sel_r[1] = dot(sel[...], qb[...]).astype(BF16)

    def link(src, dst, n, k):
        return remote(src, dst, p_send.at[n, k], p_recv.at[n, k], partner)

    give_r1 = link(rb.at[pl.ds(0, HALF)], r1_in, 0, 7)
    give_v1 = link(vb.at[pl.ds(0, HALF)], v1_in, 1, 7)

    reduce_middle(0)
    ghosts_to_one(sel_r.at[1], g_q, 0)

    valid = nbr[...] < EXT
    present = jnp.sum(jnp.where(valid, ew[...], 0.0), axis=0, keepdims=True)
    for t in range(OWN // CHUNK):
        at = slice(t * CHUNK, (t + 1) * CHUNK)
        line = present[:, at] + shift[t : t + 1, :]
        diag[at, :] = jnp.transpose(jnp.broadcast_to(line, (CHUNK, CHUNK)))
        for h in range(NB // 8):
            turned = butterfly(nbr[h * 8 : h * 8 + 8, at].astype(F32))
            turned = turned.astype(jnp.int32)
            inside = lax.broadcasted_iota(jnp.int32, (8, CHUNK), 1) % 16
            here = slice(h * CHUNK, (h + 1) * CHUNK)
            code_t[t * 8 : t * 8 + 8, here] = (turned // COLS) * 16 + inside
            base_t[t * 8 : t * 8 + 8, here] = turned % COLS
            wgt_t[t * 8 : t * 8 + 8, here] = butterfly(ew[h * 8 : h * 8 + 8, at])

    blocks = EXT // COLS
    code_row = lax.broadcasted_iota(jnp.int32, (blocks * 16, 2 * CHUNK), 0)
    base_row = lax.broadcasted_iota(jnp.int32, (COLS, 2 * CHUNK), 0)

    def build(g, _):
        one = pl.ds(g, 1)
        left = jnp.where(code_row == code_t[one, :], wgt_t[one, :], 0.0).astype(BF16)
        right = jnp.where(base_row == base_t[one, :], 1.0, 0.0).astype(BF16)
        found = dot_nt(left, right).astype(BF16)
        at = pl.ds(pl.multiple_of(g * 16, 16), 16)
        for a in range(blocks):
            w_mat[at, a * COLS : (a + 1) * COLS] = found[a * 16 : (a + 1) * 16, :]
        return 0

    groups = OWN // 16

    def fill(n, k):
        if n == 0:
            lax.fori_loop(k * groups // 4, (k + 1) * groups // 4, build, 0)
        elif k == 1:
            step_alpha = step_own[1, 0:1, :]

            def halfway(at, carry):
                value = r[at, :] - step_alpha * v[at, :]
                m[at, :] = value
                sol[at, :] = sol[at, :] + step_alpha * y_first[at, :]
                return carry + fold(s[at, :] * value)

            middle_sum[...] = chunks(halfway, zero)

    q4 = HALF // 2

    def apply(n, y):
        tail = xe.at[n, pl.ds(HALF, OWN - HALF)]
        if n == 0:
            give_x1 = link(xe.at[n, pl.ds(0, HALF)], x1_in, n, 0)
        give_tail = link(tail, tail_in.at[n], n, 1)
        give_p0 = link(p_out.at[n, 0], p_in.at[n, 0], n, 2)
        give_p1 = link(p_out.at[n, 1], p_in.at[n, 1], n, 3)
        give_u = link(u_out.at[n], u_in.at[n], n, 4)
        give_y = link(y_out.at[n], y_in.at[n], n, 5)
        give_step = link(step_own.at[n], step_in.at[n], n, 6)

        @pl.when(panel == 0)
        def _():
            give_step.start()
            give_tail.start()

            def lower(src, dst):
                for h in range(2):
                    at = slice(h * q4, (h + 1) * q4)
                    dst[at, :] = dot(low[HALF + h * q4 : HALF + (h + 1) * q4, :], src[...]).astype(BF16)

            def upper(src, put):
                inner[0:q4, :] = dot(low[0:q4, 0:q4], src[0:q4, :]).astype(BF16)
                inner[q4:HALF, :] = dot(low[q4:HALF, :], src[...]).astype(BF16)
                put(slice(0, q4), dot(up[0:q4, :], inner[...]))
                put(slice(q4, HALF), dot(up[q4:HALF, q4:HALF], inner[q4:HALF, :]))

            x1 = xe.at[n, pl.ds(0, HALF)]
            lower(x1, p_out.at[n, 0])
            give_p0.start()

            def keep(at, value):
                y[at, :] = value

            def post(at, value):
                u_out[n, at, :] = value.astype(BF16)

            if n == 0:
                upper(x1, keep)
                fill(n, 0)
                give_x1.wait_recv()
                other = x1_in
            else:
                give_r1.wait_recv()
                give_v1.wait_recv()
                give_step.wait_recv()
                x1_c[...] = (
                    r1_in[...].astype(F32) - step_in[n, 0:1, :] * v1_in[...].astype(F32)
                ).astype(BF16)
                other = x1_c
            lower(other, p_out.at[n, 1])
            give_p1.start()
            upper(other, post)
            give_u.start()
            if n == 1:
                upper(x1, keep)
            for k in (1, 2, 3):
                fill(n, k)
            give_y.wait_recv()
            for t in range(OWN // CHUNK):
                at = slice(t * CHUNK, (t + 1) * CHUNK)
                value = y_in[n, at, :].astype(F32)
                if t < HALF // CHUNK:
                    value = value + y[at, :]
                y[at, :] = value
                ub[at, :] = value.astype(BF16)
            for copy in (give_step, give_tail, give_p0, give_p1, give_u):
                copy.wait_send()

        @pl.when(panel == 1)
        def _():
            if n == 0:
                give_x1.start()
                give_r1.start()
            else:
                give_step.start()

            def extended(c, own_tail, step):
                x2_c[c, 0 : OWN - HALF, :] = own_tail
                if n == 0:
                    value = g_r[c].astype(F32) + step * g_q[c].astype(F32)
                else:
                    value = g_r[c].astype(F32) - step * g_v[c].astype(F32)
                x2_c[c, OWN - HALF : HALF, :] = value.astype(BF16)
                part[c, 0:q4, :] = dot(low[HALF : HALF + q4, 0:q4], x2_c[c, 0:q4, :])
                part[c, q4:HALF, :] = dot(low[HALF + q4 : EXT, :], x2_c[c])

            def upper(k, put):
                inner[...] = (part[k] + p_in[n, k].astype(F32)).astype(BF16)
                for h in range(2):
                    at = slice(h * (OWN // 2), (h + 1) * (OWN // 2))
                    put(at, dot(up[at, :], inner[...]))

            received = g_q if n == 0 else g_v
            fill(n, 0)
            if n == 0:
                ghosts_at_one(g_r, 2, 1)
            ghosts_at_one(received, n, 1)
            extended(1, xe[n, HALF:OWN, :], step_own[n, 0:1, :])
            if n == 0:
                ghosts_at_one(g_r, 2, 0)
            ghosts_at_one(received, n, 0)
            give_step.wait_recv()
            give_tail.wait_recv()
            extended(0, tail_in[n], step_in[n, 0:1, :])
            fill(n, 1)
            give_p0.wait_recv()

            def post(at, value):
                y_out[n, at, :] = value.astype(BF16)

            upper(0, post)
            give_y.start()
            fill(n, 2)
            give_p1.wait_recv()

            def keep(at, value):
                y[at, :] = value

            upper(1, keep)
            fill(n, 3)
            give_u.wait_recv()
            for t in range(OWN // CHUNK):
                at = slice(t * CHUNK, (t + 1) * CHUNK)
                value = y[at, :]
                if t < HALF // CHUNK:
                    value = value + u_in[n, at, :].astype(F32)
                y[at, :] = value
                ub[at, :] = value.astype(BF16)
            give_y.wait_send()
            if n == 0:
                give_x1.wait_send()
                give_r1.wait_send()
            else:
                give_step.wait_send()
                give_v1.wait_send()

    def operate(n, y, use):
        for k, peer in ((ic, far_peer), (1 - ic, near_peer)):
            mine = pl.ds(pl.multiple_of(k * BORDER, CHUNK), BORDER)
            theirs = pl.ds(pl.multiple_of((1 - k) * BORDER, CHUNK), BORDER)
            sel_u[n, mine, :] = dot(sel[mine, :], ub[...]).astype(BF16)
            send(sel_u.at[n, mine], g_u.at[n, theirs], g_send.at[n, k], g_recv.at[n, k], peer)
        v[...] = diag[...] * y[...] - dot(w_mat[:, 0:OWN], ub[...])

        def arrived(k):
            theirs = pl.ds(pl.multiple_of((1 - k) * BORDER, CHUNK), BORDER)
            remote(g_u.at[n, theirs], g_u.at[n, theirs], g_send.at[n, k], g_recv.at[n, k], partner).wait_recv()
            return g_u[n, theirs, :], pl.ds(pl.multiple_of(OWN + (1 - k) * BORDER, CHUNK), BORDER)

        rows, cols = arrived(ic)
        v[...] = v[...] - dot(w_mat[:, cols], rows)
        rows, cols = arrived(1 - ic)
        for h in range(2):
            at = slice(h * (OWN // 2), (h + 1) * (OWN // 2))
            use(at, v[at, :] - dot(w_mat[at, cols], rows))

    def whole(x):
        return jnp.sum(x, axis=0, keepdims=True)

    mean = reduce_end(0)
    rho_now, shadow_square = mean[0:1, :], mean[1:2, :]
    step_beta = rho_now / rho_prev[...] * (alpha_prev[...] / omega_before)
    step_own[0] = jnp.broadcast_to(step_beta, (8, COLS))

    def direct(at, _):
        xe[0, at, :] = (r[at, :] + step_beta * d[at, :]).astype(BF16)
        return 0

    chunks(direct)
    loads[4].wait()
    loads[5].wait()
    apply(0, y_first)

    sums = []

    def image(at, value):
        v[at, :] = value
        vb[at, :] = value.astype(BF16)
        sums.append((whole(s[at, :] * value), whole(value * value)))

    operate(0, y_first, image)
    reduce_start(1, [sums[0][i] + sums[1][i] for i in range(2)])

    @pl.when(panel == 1)
    def _():
        give_v1.start()

    sel_u[2] = dot(sel[...], vb[...]).astype(BF16)
    loads[6].wait()
    reduce_middle(1)
    ghosts_to_one(sel_u.at[2], g_v, 1)
    mean = reduce_end(1)
    denominator, image_square = mean[0:1, :], mean[1:2, :]
    step_alpha = rho_now / jnp.maximum(
        denominator, FLOOR_SHARE * jnp.sqrt(shadow_square * image_square)
    )
    step_own[1] = jnp.broadcast_to(step_alpha, (8, COLS))

    def middle(at, _):
        xe[1, at, :] = (r[at, :] - step_alpha * v[at, :]).astype(BF16)
        return 0

    chunks(middle)
    apply(1, y_second)
    store = [load(sol, sol_out, 7), load(m, m_out, 8), load(y_second, y_out_hbm, 9)]
    sums = []

    def test(at, value):
        v[at, :] = value
        sums.append((whole(value * m[at, :]), whole(value * value), whole(s[at, :] * value)))

    operate(1, y_second, test)
    store.append(load(v, t_out, 10))
    tm, tt, st = (sums[0][i] + sums[1][i] for i in range(3))
    reduce_start(2, [tm, tt, whole(middle_sum[...]), st])
    reduce_middle(2)
    mean = reduce_end(2)
    stats[...] = jnp.concatenate([mean[0:4, :], step_alpha, jnp.zeros((3, COLS), F32)], axis=0)
    for copy in store:
        copy.wait()
    for copy in sends:
        copy.wait_send()


def finish(sol, y, m, t, stats, new_sol, new_res, alpha, omega, rho):
    step_omega = stats[0:1, :] / (stats[1:2, :] + EPSILON)
    new_sol[...] = sol[...] + step_omega * y[...]
    new_res[...] = m[...] - step_omega * t[...]
    alpha[...] = stats[4:5, :]
    omega[...] = step_omega
    rho[...] = stats[2:3, :] - step_omega * stats[3:4, :]


def per_device(
    solution, residual, shadow, direction, old_image, rho_prev, alpha_prev, omega_prev,
    lower_inverse, upper_inverse, neighbours, edge_weight, node_shift, send_rows,
):
    hbm = pl.BlockSpec(memory_space=pl.ANY)
    vmem = pl.BlockSpec(memory_space=pltpu.VMEM)
    dma = pltpu.SemaphoreType.DMA

    def f32(*shape):
        return pltpu.VMEM(shape, F32)

    def b16(*shape):
        return pltpu.VMEM(shape, BF16)

    def row(x):
        return x.reshape(1, COLS)

    array = jax.ShapeDtypeStruct((OWN, COLS), F32)
    line = jax.ShapeDtypeStruct((1, COLS), F32)
    vec = f32(OWN, COLS)
    tables = [pltpu.VMEM((OWN // 16, 256), kind) for kind in (jnp.int32, jnp.int32, F32)]
    parts = pl.pallas_call(
        kernel,
        out_shape=[array] * 4 + [jax.ShapeDtypeStruct((8, COLS), F32)],
        in_specs=[hbm] * 7 + [vmem] * 7,
        out_specs=[hbm] * 4 + [vmem],
        scratch_shapes=[vec] * 5
        + [b16(EXT, HALF), b16(OWN, HALF)]
        + [b16(OWN, EXT), b16(2 * BORDER, OWN), vec] + tables
        + [
            b16(2, OWN, COLS), b16(OWN, COLS), b16(OWN, COLS), b16(2, 2 * BORDER, COLS),
            b16(2, 2 * BORDER, COLS), b16(2, 2 * BORDER, COLS), b16(3, 2 * BORDER, COLS), b16(2, 2 * BORDER, COLS),
            b16(2, 2 * BORDER, COLS), b16(OWN, COLS), b16(OWN, COLS), vec, vec, vec, vec,
        ]
        + [
            b16(HALF, COLS), b16(HALF, COLS), b16(HALF, COLS), b16(2, OWN - HALF, COLS),
            b16(2, 2, HALF, COLS), b16(2, HALF, COLS), b16(2, OWN, COLS),
            b16(2, 2, HALF, COLS), b16(2, HALF, COLS), b16(2, OWN, COLS),
            b16(HALF, COLS), f32(2, HALF, COLS), b16(HALF, COLS), b16(2, HALF, COLS),
        ]
        + [f32(2, 8, COLS), f32(2, 8, COLS), f32(8, COLS)]
        + [f32(k, rows, COLS) for rows in (2, 2, 4) for k in (NX * NY, NZ * NC)]
        + [
            dma((11,)), dma((2, 2)), dma((2, 2)), dma((3, 2)), dma((3, 2, 2)),
            dma((2, 8)), dma((2, 8)), dma((3, 2)), dma((3, 2)),
        ],
        compiler_params=pltpu.CompilerParams(
            collective_id=0, has_side_effects=True, vmem_limit_bytes=60 * 1024 * 1024
        ),
        name="iteration",
    )(
        residual, shadow, direction, old_image, solution, lower_inverse, upper_inverse,
        row(rho_prev), row(alpha_prev), row(omega_prev),
        neighbours, edge_weight, node_shift.reshape(OWN // CHUNK, CHUNK), send_rows,
    )
    steps = 1
    block = pl.BlockSpec((OWN // steps, COLS), lambda i: (i, 0))
    fixed = pl.BlockSpec((1, COLS), lambda i: (0, 0))
    new_solution, new_residual, alpha, omega, rho = pl.pallas_call(
        finish,
        out_shape=[array] * 2 + [line] * 3,
        grid=(steps,),
        in_specs=[block] * 4 + [pl.BlockSpec((8, COLS), lambda i: (0, 0))],
        out_specs=[block] * 2 + [fixed] * 3,
        name="finish",
    )(*parts)
    return new_solution, new_residual, alpha[0], omega[0], rho[0]


def solution(mesh):
    torus = Mesh(
        mesh.devices.reshape(4, 4, 4, 2, mesh.shape["panel"]),
        ("sub_0", "sub_1", "sub_2", "sub_3", "panel"),
    )
    vec = P(SUB, "panel")
    one = P("panel")
    factor = P(SUB, None, "panel")
    in_specs = (
        vec, vec, vec, vec, vec, one, one, one, factor, factor,
        P(None, SUB), P(None, SUB), P(SUB), P(SUB, None, None),
    )
    return jax.shard_map(
        per_device, mesh=torus, in_specs=in_specs, out_specs=(vec, vec, one, one, one), check_vma=False
    )
```

```python
import functools

import jax
import jax.numpy as jnp
from jax import lax
from jax.experimental import pallas as pl
from jax.experimental.pallas import tpu as pltpu
from jax.sharding import Mesh
from jax.sharding import PartitionSpec as P

SUB = ("sub_0", "sub_1", "sub_2", "sub_3")
FLOOR_SHARE = 0.3
EPSILON = 1e-06

OWN = 1024
EXT = 1792
HALF = 896
BORDER = 384
NB = 16
COLS = 128
CHUNK = 128
NX, NY, NZ, NC = 4, 4, 4, 2
F32 = jnp.float32
BF16 = jnp.bfloat16
MESH = pl.DeviceIdType.MESH


def dot(a, b):
    return lax.dot_general(a, b, (((1,), (0,)), ((), ())), preferred_element_type=F32)


def dot_nt(a, b):
    return lax.dot_general(a, b, (((1,), (1,)), ((), ())), preferred_element_type=F32)


def chunks(body, init=0):
    def step(i, carry):
        return body(pl.ds(pl.multiple_of(i * CHUNK, CHUNK), CHUNK), carry)

    return lax.fori_loop(0, OWN // CHUNK, step, init, unroll=True)


def fold(x):
    return jnp.sum(x.reshape(CHUNK // 8, 8, COLS), axis=0)


def butterfly(x):
    sub = lax.broadcasted_iota(jnp.int32, x.shape, 0)
    lane = lax.broadcasted_iota(jnp.int32, x.shape, 1) // 16
    for s in (1, 2, 4):
        down = pltpu.roll(pltpu.roll(x, s, 0), 128 - 16 * s, 1)
        up = pltpu.roll(pltpu.roll(x, 8 - s, 0), 16 * s, 1)
        sub_bit = (sub // s) % 2
        lane_bit = (lane // s) % 2
        x = jnp.where(sub_bit == lane_bit, x, jnp.where(sub_bit == 1, down, up))
    return x


def kernel(
    r_hbm, s_hbm, d_hbm, oi_hbm, sol_hbm, low_hbm, up_hbm,
    rho_prev, alpha_prev, omega_prev, nbr, ew, shift, rows_ref,
    sol_out, y_out_hbm, m_out, t_out, stats,
    r, s, d, oi, sol, low, up,
    w_mat, sel, diag, code_t, base_t, wgt_t,
    xe, rb, qb, sel_r, g_r, g_q, sel_u, g_u, g_v, ub, vb, y_first, y_second, v, m,
    x1_in, r1_in, v1_in, tail_in, p_in, u_in, y_in, p_out, u_out, y_out, inner, part, x1_c, x2_c,
    step_own, step_in, middle_sum, red_a0, red_b0, red_a1, red_b1, red_a2, red_b2,
    load_sem, g_send, g_recv, h_send, h_recv, p_send, p_recv, a_send, a_recv,
):
    panel = lax.axis_index("panel")
    ix, iy, iz, ic = (lax.axis_index(name) for name in SUB)
    flat = ((ix * NY + iy) * NZ + iz) * NC + ic

    def coords(index):
        return {
            "sub_0": index // (NY * NZ * NC),
            "sub_1": (index // (NZ * NC)) % NY,
            "sub_2": (index // NC) % NZ,
            "sub_3": index % NC,
        }

    total = NX * NY * NZ * NC
    above = coords((flat + 1) % total)
    below = coords((flat + total - 1) % total)
    far_peer = coords((flat + total + 2 * ic - 1) % total)
    near_peer = coords((flat + total + 1 - 2 * ic) % total)
    above_one = {**above, "panel": 1}
    below_one = {**below, "panel": 1}
    partner = {"panel": 1 - panel}
    plane = [
        {"sub_0": (ix + o // NY) % NX, "sub_1": (iy + o % NY) % NY} for o in range(1, NX * NY)
    ]
    column = [
        {"sub_2": (iz + o // NC) % NZ, "sub_3": (ic + o % NC) % NC} for o in range(1, NZ * NC)
    ]

    def load(src, dst, i):
        copy = pltpu.make_async_copy(src, dst, load_sem.at[i])
        copy.start()
        return copy

    loads = [
        load(s_hbm, s, 0), load(r_hbm, r, 1), load(d_hbm, d, 2), load(oi_hbm, oi, 3),
    ]

    barrier = pltpu.get_barrier_semaphore()
    peers = plane + column + [
        above, below, {**above, "panel": 1 - panel}, {**below, "panel": 1 - panel}, partner,
    ]
    for peer in peers:
        pl.semaphore_signal(barrier, inc=1, device_id=peer, device_id_type=MESH)

    sends = []

    def remote(src, dst, ssem, rsem, peer):
        return pltpu.make_async_remote_copy(
            src_ref=src, dst_ref=dst, send_sem=ssem, recv_sem=rsem,
            device_id=peer, device_id_type=MESH,
        )

    def send(src, dst, ssem, rsem, peer):
        copy = remote(src, dst, ssem, rsem, peer)
        copy.start()
        sends.append(copy)

    red_a, red_b = (red_a0, red_a1, red_a2), (red_b0, red_b1, red_b2)

    def all_of(buf, n, stage, count):
        every = buf.at[pl.ds(0, count)]
        return remote(every, every, a_send.at[n, stage], a_recv.at[n, stage], partner)

    def reduce_start(n, rows):
        mine = red_a[n].at[ix * NY + iy]
        mine[...] = jnp.concatenate(rows, axis=0)
        for peer in plane:
            remote(mine, mine, a_send.at[n, 0], a_recv.at[n, 0], peer).start()
        sends.append(all_of(red_a[n], n, 0, NX * NY - 1))

    def reduce_middle(n):
        all_of(red_a[n], n, 0, NX * NY - 1).wait_recv()
        mine = red_b[n].at[iz * NC + ic]
        mine[...] = jnp.sum(red_a[n][...], axis=0)
        for peer in column:
            remote(mine, mine, a_send.at[n, 1], a_recv.at[n, 1], peer).start()
        sends.append(all_of(red_b[n], n, 1, NZ * NC - 1))

    def reduce_end(n):
        all_of(red_b[n], n, 1, NZ * NC - 1).wait_recv()
        return jnp.sum(red_b[n][...], axis=0) * (1.0 / (OWN * total))

    low_rows, high_rows = pl.ds(0, BORDER), pl.ds(BORDER, BORDER)

    def ghosts_to_one(src, dst, k):
        send(src.at[low_rows], dst.at[panel, high_rows], h_send.at[k, 0], h_recv.at[k, panel, 0], below_one)
        send(src.at[high_rows], dst.at[panel, low_rows], h_send.at[k, 1], h_recv.at[k, panel, 1], above_one)

    def ghosts_at_one(dst, k, c):
        remote(dst.at[c, high_rows], dst.at[c, high_rows], h_send.at[k, 0], h_recv.at[k, c, 0], partner).wait_recv()
        remote(dst.at[c, low_rows], dst.at[c, low_rows], h_send.at[k, 1], h_recv.at[k, c, 1], partner).wait_recv()

    zero = jnp.zeros((8, COLS), F32)

    lane = lax.broadcasted_iota(jnp.int32, (CHUNK, CHUNK), 1).astype(F32)
    for n in range(2 * BORDER // CHUNK):
        side, at = n // (BORDER // CHUNK), (n % (BORDER // CHUNK)) * CHUNK
        chosen = rows_ref[0, side : side + 1, at : at + CHUNK].astype(F32)
        across = jnp.transpose(jnp.broadcast_to(chosen, (CHUNK, CHUNK)))
        for t in range(OWN // CHUNK):
            sel[n * CHUNK : (n + 1) * CHUNK, t * CHUNK : (t + 1) * CHUNK] = jnp.where(
                across == lane + float(t * CHUNK), 1.0, 0.0
            ).astype(BF16)

    loads[0].wait()
    loads[1].wait()
    loads.extend([
        load(low_hbm.at[0], low, 4), load(up_hbm.at[0, pl.ds(0, OWN)], up, 5), load(sol_hbm, sol, 6),
    ])

    def opening(at, carry):
        sr, ss = carry
        a, b = s[at, :], r[at, :]
        rb[at, :] = b.astype(BF16)
        return sr + fold(a * b), ss + fold(a * a)

    sr, ss = chunks(opening, (zero, zero))
    sel_r[0] = dot(sel[...], rb[...]).astype(BF16)
    pl.semaphore_wait(barrier, len(peers))
    reduce_start(0, [jnp.sum(sr, axis=0, keepdims=True), jnp.sum(ss, axis=0, keepdims=True)])
    ghosts_to_one(sel_r.at[0], g_r, 2)

    loads[2].wait()
    loads[3].wait()
    omega_before = omega_prev[...]

    def combine(at, _):
        q = d[at, :] - omega_before * oi[at, :]
        d[at, :] = q
        qb[at, :] = q.astype(BF16)
        return 0

    chunks(combine)
    sel_r[1] = dot(sel[...], qb[...]).astype(BF16)

    def link(src, dst, n, k):
        return remote(src, dst, p_send.at[n, k], p_recv.at[n, k], partner)

    give_r1 = link(rb.at[pl.ds(0, HALF)], r1_in, 0, 7)
    give_v1 = link(vb.at[pl.ds(0, HALF)], v1_in, 1, 7)

    reduce_middle(0)
    ghosts_to_one(sel_r.at[1], g_q, 0)

    valid = nbr[...] < EXT
    present = jnp.sum(jnp.where(valid, ew[...], 0.0), axis=0, keepdims=True)
    for t in range(OWN // CHUNK):
        at = slice(t * CHUNK, (t + 1) * CHUNK)
        line = present[:, at] + shift[t : t + 1, :]
        diag[at, :] = jnp.transpose(jnp.broadcast_to(line, (CHUNK, CHUNK)))
        for h in range(NB // 8):
            turned = butterfly(nbr[h * 8 : h * 8 + 8, at].astype(F32))
            turned = turned.astype(jnp.int32)
            inside = lax.broadcasted_iota(jnp.int32, (8, CHUNK), 1) % 16
            here = slice(h * CHUNK, (h + 1) * CHUNK)
            code_t[t * 8 : t * 8 + 8, here] = (turned // COLS) * 16 + inside
            base_t[t * 8 : t * 8 + 8, here] = turned % COLS
            wgt_t[t * 8 : t * 8 + 8, here] = butterfly(ew[h * 8 : h * 8 + 8, at])

    blocks = EXT // COLS
    code_row = lax.broadcasted_iota(jnp.int32, (blocks * 16, 2 * CHUNK), 0)
    base_row = lax.broadcasted_iota(jnp.int32, (COLS, 2 * CHUNK), 0)

    def build(g, _):
        one = pl.ds(g, 1)
        left = jnp.where(code_row == code_t[one, :], wgt_t[one, :], 0.0).astype(BF16)
        right = jnp.where(base_row == base_t[one, :], 1.0, 0.0).astype(BF16)
        found = dot_nt(left, right).astype(BF16)
        at = pl.ds(pl.multiple_of(g * 16, 16), 16)
        for a in range(blocks):
            w_mat[at, a * COLS : (a + 1) * COLS] = found[a * 16 : (a + 1) * 16, :]
        return 0

    groups, part_size = OWN // 16, 13
    early = groups - 4 * part_size
    lax.fori_loop(0, early, build, 0)

    def fill(n, k):
        if n == 0:
            lax.fori_loop(early + k * part_size, early + (k + 1) * part_size, build, 0)
        elif k == 1:
            step_alpha = step_own[1, 0:1, :]

            def halfway(at, carry):
                value = r[at, :] - step_alpha * v[at, :]
                m[at, :] = value
                sol[at, :] = sol[at, :] + step_alpha * y_first[at, :]
                return carry + fold(s[at, :] * value)

            middle_sum[...] = chunks(halfway, zero)

    q4 = HALF // 2

    def apply(n, y):
        tail = xe.at[n, pl.ds(HALF, OWN - HALF)]
        if n == 0:
            give_x1 = link(xe.at[n, pl.ds(0, HALF)], x1_in, n, 0)
        give_tail = link(tail, tail_in.at[n], n, 1)
        give_p0 = link(p_out.at[n, 0], p_in.at[n, 0], n, 2)
        give_p1 = link(p_out.at[n, 1], p_in.at[n, 1], n, 3)
        give_u = link(u_out.at[n], u_in.at[n], n, 4)
        give_y = link(y_out.at[n], y_in.at[n], n, 5)
        give_step = link(step_own.at[n], step_in.at[n], n, 6)

        @pl.when(panel == 0)
        def _():
            give_step.start()
            give_tail.start()

            def lower(src, dst):
                for h in range(2):
                    at = slice(h * q4, (h + 1) * q4)
                    dst[at, :] = dot(low[HALF + h * q4 : HALF + (h + 1) * q4, :], src[...]).astype(BF16)

            def upper(src, put):
                inner[0:q4, :] = dot(low[0:q4, 0:q4], src[0:q4, :]).astype(BF16)
                inner[q4:HALF, :] = dot(low[q4:HALF, :], src[...]).astype(BF16)
                put(slice(0, q4), dot(up[0:q4, :], inner[...]))
                put(slice(q4, HALF), dot(up[q4:HALF, q4:HALF], inner[q4:HALF, :]))

            x1 = xe.at[n, pl.ds(0, HALF)]
            lower(x1, p_out.at[n, 0])
            give_p0.start()

            def keep(at, value):
                y[at, :] = value

            def post(at, value):
                u_out[n, at, :] = value.astype(BF16)

            if n == 0:
                upper(x1, keep)
                fill(n, 0)
                give_x1.wait_recv()
                other = x1_in
            else:
                give_r1.wait_recv()
                give_v1.wait_recv()
                give_step.wait_recv()
                x1_c[...] = (
                    r1_in[...].astype(F32) - step_in[n, 0:1, :] * v1_in[...].astype(F32)
                ).astype(BF16)
                other = x1_c
            lower(other, p_out.at[n, 1])
            give_p1.start()
            upper(other, post)
            give_u.start()
            if n == 1:
                upper(x1, keep)
            for k in (1, 2, 3):
                fill(n, k)
            give_y.wait_recv()
            for t in range(OWN // CHUNK):
                at = slice(t * CHUNK, (t + 1) * CHUNK)
                value = y_in[n, at, :].astype(F32)
                if t < HALF // CHUNK:
                    value = value + y[at, :]
                y[at, :] = value
                ub[at, :] = value.astype(BF16)
            for copy in (give_step, give_tail, give_p0, give_p1, give_u):
                copy.wait_send()

        @pl.when(panel == 1)
        def _():
            if n == 0:
                give_x1.start()
                give_r1.start()
            else:
                give_step.start()

            def extended(c, own_tail, step):
                x2_c[c, 0 : OWN - HALF, :] = own_tail
                if n == 0:
                    value = g_r[c].astype(F32) + step * g_q[c].astype(F32)
                else:
                    value = g_r[c].astype(F32) - step * g_v[c].astype(F32)
                x2_c[c, OWN - HALF : HALF, :] = value.astype(BF16)
                part[c, 0:q4, :] = dot(low[HALF : HALF + q4, 0:q4], x2_c[c, 0:q4, :])
                part[c, q4:HALF, :] = dot(low[HALF + q4 : EXT, :], x2_c[c])

            def upper(k, put):
                inner[...] = (part[k] + p_in[n, k].astype(F32)).astype(BF16)
                for h in range(2):
                    at = slice(h * (OWN // 2), (h + 1) * (OWN // 2))
                    put(at, dot(up[at, :], inner[...]))

            received = g_q if n == 0 else g_v
            fill(n, 0)
            if n == 0:
                ghosts_at_one(g_r, 2, 1)
            ghosts_at_one(received, n, 1)
            extended(1, xe[n, HALF:OWN, :], step_own[n, 0:1, :])
            if n == 0:
                ghosts_at_one(g_r, 2, 0)
            ghosts_at_one(received, n, 0)
            give_step.wait_recv()
            give_tail.wait_recv()
            extended(0, tail_in[n], step_in[n, 0:1, :])
            fill(n, 1)
            give_p0.wait_recv()

            def post(at, value):
                y_out[n, at, :] = value.astype(BF16)

            upper(0, post)
            give_y.start()
            fill(n, 2)
            give_p1.wait_recv()

            def keep(at, value):
                y[at, :] = value

            upper(1, keep)
            fill(n, 3)
            give_u.wait_recv()
            for t in range(OWN // CHUNK):
                at = slice(t * CHUNK, (t + 1) * CHUNK)
                value = y[at, :]
                if t < HALF // CHUNK:
                    value = value + u_in[n, at, :].astype(F32)
                y[at, :] = value
                ub[at, :] = value.astype(BF16)
            give_y.wait_send()
            if n == 0:
                give_x1.wait_send()
                give_r1.wait_send()
            else:
                give_step.wait_send()
                give_v1.wait_send()

    def operate(n, y, use):
        for k, peer in ((ic, far_peer), (1 - ic, near_peer)):
            mine = pl.ds(pl.multiple_of(k * BORDER, CHUNK), BORDER)
            theirs = pl.ds(pl.multiple_of((1 - k) * BORDER, CHUNK), BORDER)
            sel_u[n, mine, :] = dot(sel[mine, :], ub[...]).astype(BF16)
            send(sel_u.at[n, mine], g_u.at[n, theirs], g_send.at[n, k], g_recv.at[n, k], peer)
        v[...] = diag[...] * y[...] - dot(w_mat[:, 0:OWN], ub[...])

        def arrived(k):
            theirs = pl.ds(pl.multiple_of((1 - k) * BORDER, CHUNK), BORDER)
            remote(g_u.at[n, theirs], g_u.at[n, theirs], g_send.at[n, k], g_recv.at[n, k], partner).wait_recv()
            return g_u[n, theirs, :], pl.ds(pl.multiple_of(OWN + (1 - k) * BORDER, CHUNK), BORDER)

        rows, cols = arrived(ic)
        v[...] = v[...] - dot(w_mat[:, cols], rows)
        rows, cols = arrived(1 - ic)
        for h in range(2):
            at = slice(h * (OWN // 2), (h + 1) * (OWN // 2))
            use(at, v[at, :] - dot(w_mat[at, cols], rows))

    def whole(x):
        return jnp.sum(x, axis=0, keepdims=True)

    mean = reduce_end(0)
    rho_now, shadow_square = mean[0:1, :], mean[1:2, :]
    step_beta = rho_now / rho_prev[...] * (alpha_prev[...] / omega_before)
    step_own[0] = jnp.broadcast_to(step_beta, (8, COLS))

    def direct(at, _):
        xe[0, at, :] = (r[at, :] + step_beta * d[at, :]).astype(BF16)
        return 0

    chunks(direct)
    loads[4].wait()
    loads[5].wait()
    apply(0, y_first)

    sums = []

    def image(at, value):
        v[at, :] = value
        vb[at, :] = value.astype(BF16)
        sums.append((whole(s[at, :] * value), whole(value * value)))

    operate(0, y_first, image)
    reduce_start(1, [sums[0][i] + sums[1][i] for i in range(2)])

    @pl.when(panel == 1)
    def _():
        give_v1.start()

    sel_u[2] = dot(sel[...], vb[...]).astype(BF16)
    loads[6].wait()
    reduce_middle(1)
    ghosts_to_one(sel_u.at[2], g_v, 1)
    mean = reduce_end(1)
    denominator, image_square = mean[0:1, :], mean[1:2, :]
    step_alpha = rho_now / jnp.maximum(
        denominator, FLOOR_SHARE * jnp.sqrt(shadow_square * image_square)
    )
    step_own[1] = jnp.broadcast_to(step_alpha, (8, COLS))

    def middle(at, _):
        xe[1, at, :] = (r[at, :] - step_alpha * v[at, :]).astype(BF16)
        return 0

    chunks(middle)
    apply(1, y_second)
    store = [load(sol, sol_out, 7), load(m, m_out, 8), load(y_second, y_out_hbm, 9)]
    sums = []

    def test(at, value):
        v[at, :] = value
        sums.append((whole(value * m[at, :]), whole(value * value), whole(s[at, :] * value)))

    operate(1, y_second, test)
    store.append(load(v, t_out, 10))
    tm, tt, st = (sums[0][i] + sums[1][i] for i in range(3))
    reduce_start(2, [tm, tt, whole(middle_sum[...]), st])
    reduce_middle(2)
    mean = reduce_end(2)
    stats[...] = jnp.concatenate([mean[0:4, :], step_alpha, jnp.zeros((3, COLS), F32)], axis=0)
    for copy in store:
        copy.wait()
    for copy in sends:
        copy.wait_send()


def finish(sol, y, m, t, stats, new_sol, new_res, alpha, omega, rho):
    step_omega = stats[0:1, :] / (stats[1:2, :] + EPSILON)
    new_sol[...] = sol[...] + step_omega * y[...]
    new_res[...] = m[...] - step_omega * t[...]
    alpha[...] = stats[4:5, :]
    omega[...] = step_omega
    rho[...] = stats[2:3, :] - step_omega * stats[3:4, :]


def per_device(
    solution, residual, shadow, direction, old_image, rho_prev, alpha_prev, omega_prev,
    lower_inverse, upper_inverse, neighbours, edge_weight, node_shift, send_rows,
):
    hbm = pl.BlockSpec(memory_space=pl.ANY)
    vmem = pl.BlockSpec(memory_space=pltpu.VMEM)
    dma = pltpu.SemaphoreType.DMA

    def f32(*shape):
        return pltpu.VMEM(shape, F32)

    def b16(*shape):
        return pltpu.VMEM(shape, BF16)

    def row(x):
        return x.reshape(1, COLS)

    array = jax.ShapeDtypeStruct((OWN, COLS), F32)
    line = jax.ShapeDtypeStruct((1, COLS), F32)
    vec = f32(OWN, COLS)
    tables = [pltpu.VMEM((OWN // 16, 256), kind) for kind in (jnp.int32, jnp.int32, F32)]
    parts = pl.pallas_call(
        kernel,
        out_shape=[array] * 4 + [jax.ShapeDtypeStruct((8, COLS), F32)],
        in_specs=[hbm] * 7 + [vmem] * 7,
        out_specs=[hbm] * 4 + [vmem],
        scratch_shapes=[vec] * 5
        + [b16(EXT, HALF), b16(OWN, HALF)]
        + [b16(OWN, EXT), b16(2 * BORDER, OWN), vec] + tables
        + [
            b16(2, OWN, COLS), b16(OWN, COLS), b16(OWN, COLS), b16(2, 2 * BORDER, COLS),
            b16(2, 2 * BORDER, COLS), b16(2, 2 * BORDER, COLS), b16(3, 2 * BORDER, COLS), b16(2, 2 * BORDER, COLS),
            b16(2, 2 * BORDER, COLS), b16(OWN, COLS), b16(OWN, COLS), vec, vec, vec, vec,
        ]
        + [
            b16(HALF, COLS), b16(HALF, COLS), b16(HALF, COLS), b16(2, OWN - HALF, COLS),
            b16(2, 2, HALF, COLS), b16(2, HALF, COLS), b16(2, OWN, COLS),
            b16(2, 2, HALF, COLS), b16(2, HALF, COLS), b16(2, OWN, COLS),
            b16(HALF, COLS), f32(2, HALF, COLS), b16(HALF, COLS), b16(2, HALF, COLS),
        ]
        + [f32(2, 8, COLS), f32(2, 8, COLS), f32(8, COLS)]
        + [f32(k, rows, COLS) for rows in (2, 2, 4) for k in (NX * NY, NZ * NC)]
        + [
            dma((11,)), dma((2, 2)), dma((2, 2)), dma((3, 2)), dma((3, 2, 2)),
            dma((2, 8)), dma((2, 8)), dma((3, 2)), dma((3, 2)),
        ],
        compiler_params=pltpu.CompilerParams(
            collective_id=0, has_side_effects=True, vmem_limit_bytes=60 * 1024 * 1024
        ),
        name="iteration",
    )(
        residual, shadow, direction, old_image, solution, lower_inverse, upper_inverse,
        row(rho_prev), row(alpha_prev), row(omega_prev),
        neighbours, edge_weight, node_shift.reshape(OWN // CHUNK, CHUNK), send_rows,
    )
    steps = 1
    block = pl.BlockSpec((OWN // steps, COLS), lambda i: (i, 0))
    fixed = pl.BlockSpec((1, COLS), lambda i: (0, 0))
    new_solution, new_residual, alpha, omega, rho = pl.pallas_call(
        finish,
        out_shape=[array] * 2 + [line] * 3,
        grid=(steps,),
        in_specs=[block] * 4 + [pl.BlockSpec((8, COLS), lambda i: (0, 0))],
        out_specs=[block] * 2 + [fixed] * 3,
        name="finish",
    )(*parts)
    return new_solution, new_residual, alpha[0], omega[0], rho[0]


def solution(mesh):
    torus = Mesh(
        mesh.devices.reshape(4, 4, 4, 2, mesh.shape["panel"]),
        ("sub_0", "sub_1", "sub_2", "sub_3", "panel"),
    )
    vec = P(SUB, "panel")
    one = P("panel")
    factor = P(SUB, None, "panel")
    in_specs = (
        vec, vec, vec, vec, vec, one, one, one, factor, factor,
        P(None, SUB), P(None, SUB), P(SUB), P(SUB, None, None),
    )
    return jax.shard_map(
        per_device, mesh=torus, in_specs=in_specs, out_specs=(vec, vec, one, one, one), check_vma=False
    )
```
